256 devices in a mesh: blk: 32 (over y_lo, z, core), head: 8 (over x, y_hi).
Axes of the slice: x: 4, y: 4 (y_hi: 2, y_lo: 2; y = y_hi * 2 + y_lo), z: 8, core: 2. Of those that a mesh axis runs over, the one named last changes fastest.
Arguments:
- pages: bfloat16 [32, 16, 16, 768], P('blk'), may hold values from -6 to 6
- valid_counts: int32 [32], replicated, may hold values from 32 to 256
- dw_weight: float32 [7, 7, 768], replicated, may hold values from -0.875 to 0.875
- dw_bias: float32 [768], replicated, may hold values from -3 to 3
- norm1_gain: float32 [768], replicated, may hold values from 0.5 to 2
- fc1_w: bfloat16 [768, 3072], P(None, 'head'), may hold values from -0.21875 to 0.21875
- fc1_b: float32 [3072], P('head'), may hold values from -3 to 3
- fc2_w: bfloat16 [3072, 768], P('head'), may hold values from -0.109375 to 0.109375
- fc2_b: float32 [768], replicated, may hold values from -3 to 3
- layer_scale: float32 [768], replicated, may hold values from 0.5 to 2
- norm2_gain: float32 [768], replicated, may hold values from 0.5 to 2
- w_query: bfloat16 [768, 4096], P(None, 'head'), may hold values from -3 to 3
- w_key: bfloat16 [768, 1024], P(None, 'head'), may hold values from -0.21875 to 0.21875
- w_value: bfloat16 [768, 1024], P(None, 'head'), may hold values from -0.21875 to 0.21875
- w_out: bfloat16 [4096, 768], P('head'), may hold values from -0.09375 to 0.09375
Outputs:
- mixed: bfloat16 [8192, 768], P(('blk', 'head'))
The draws below stay inside these ranges and needn't reach their ends.
All inputs are finite; a program needn't handle non-finite values.
Results may differ from the reference program's by a relative error of at most 0.023.
Values may be sent and summed in bfloat16 or wider, within the bound.
No kernel may reach another device: no remote copies, remote signals or barrier semaphores. Data moves between devices by JAX's collectives and lax.ppermute only.
A program may use at most 128 MiB of HBM per device.

```python
import math
import jax
import jax.numpy as jnp
from jax import lax

C = 768
HID = 3072
HEADS = 32
KV_HEADS = 8
HD = 128
GH = 16
GW = 16
PAGES = 32


def draw_w_query(key, part):
    columns = HEADS * HD
    drawn = jax.random.normal(key, (C, columns), jnp.float32) * (3.0 / math.sqrt(C))
    return jnp.clip(drawn, -3.0, 3.0).astype(jnp.bfloat16)


def place_ends(array, rng, smallest, high):
    longest = array.shape.index(max(array.shape))
    spots = []
    for shift in (0, 1):
        where = [jax.random.randint(jax.random.fold_in(rng, axis), (), 0, length) for axis, length in enumerate(array.shape)]
        where[longest] = (where[longest] + shift) % array.shape[longest]
        spots.append(tuple(where))
    return array.at[spots[0]].set(smallest).at[spots[1]].set(high)


def shard_levels(stream_key, shape, cuts, low, top_value):
    loudness, own = 1.0, jax.random.fold_in(stream_key, 6)
    for axis_at, blocks in cuts:
        steps = jnp.exp(jax.random.uniform(jax.random.fold_in(own, axis_at), (blocks,), jnp.float32, low / len(cuts), top_value / len(cuts)))
        loudness = loudness * jnp.repeat(steps, shape[axis_at] // blocks).reshape([-1 if axis == axis_at else 1 for axis in range(len(shape))])
    return loudness


def noise(stream_key, dims, deviation, most, cuts=(), kind=jnp.bfloat16):
    array = jax.random.normal(stream_key, dims, jnp.float32) * deviation
    if len(cuts) > 0:
        array = shard_levels(stream_key, dims, cuts, -0.22, 0.18) * array
    return jnp.clip(array, min=-most, max=most).astype(kind)


def setup_inputs(seed: int = 0) -> dict:
    key_list = jax.random.split(jax.random.key(seed), 16)
    return {
        "pages": noise(key_list[0], (PAGES, GH, GW, C), 1.0, 6.0, ((0, 32),)),
        "valid_counts": place_ends(jax.random.randint(key_list[1], (PAGES,), GH * GW // 8, GH * GW + 1), jax.random.fold_in(key_list[1], 1), GH * GW // 8, GH * GW).astype(jnp.int32),
        "dw_weight": noise(key_list[2], (7, 7, C), 49 ** -0.5, 0.875, (), jnp.float32),
        "dw_bias": noise(key_list[3], (C,), 0.5, 3.0, (), jnp.float32),
        "norm1_gain": jnp.clip(jnp.exp(jax.random.uniform(key_list[4], (C,), jnp.float32, math.log(0.5), math.log(2.0))), 0.5, 2.0),
        "fc1_w": noise(key_list[5], (C, HID), C ** -0.5, 0.21875, ((1, 8),)),
        "fc1_b": noise(key_list[6], (HID,), 0.5, 3.0, ((0, 8),), jnp.float32),
        "fc2_w": noise(key_list[7], (HID, C), HID ** -0.5, 0.109375, ((0, 8),)),
        "fc2_b": noise(key_list[8], (C,), 0.5, 3.0, (), jnp.float32),
        "layer_scale": jnp.clip(jnp.exp(jax.random.uniform(key_list[9], (C,), jnp.float32, math.log(0.5), math.log(2.0))), 0.5, 2.0),
        "norm2_gain": jnp.clip(jnp.exp(jax.random.uniform(key_list[10], (C,), jnp.float32, math.log(0.5), math.log(2.0))), 0.5, 2.0),
        "w_query": draw_w_query(jax.random.fold_in(key_list[15], 71), 0),
        "w_key": noise(key_list[12], (C, KV_HEADS * HD), C ** -0.5, 0.21875, ((1, 8),)),
        "w_value": noise(key_list[13], (C, KV_HEADS * HD), C ** -0.5, 0.21875, ((1, 8),)),
        "w_out": noise(key_list[14], (HEADS * HD, C), (HEADS * HD) ** -0.5, 0.09375, ((0, 8),)),
    }


def depthwise(pages, dw_weight, dw_bias):
    height = pages.shape[1]
    breadth = pages.shape[2]
    padded = jnp.pad(pages.astype(jnp.float32), ((0, 0), (3, 3), (3, 3), (0, 0)))
    total = jnp.zeros(pages.shape, jnp.float32)
    for vertical in range(7):
        for sideways in range(7):
            total = total + padded[:, vertical:vertical + height, sideways:sideways + breadth, :] * dw_weight[vertical, sideways]
    return total + dw_bias

def layer_norm(values, gain, epsilon):
    centred = values - lax.optimization_barrier(jnp.mean(values, axis=-1, keepdims=True))
    spread = lax.optimization_barrier(jnp.mean(centred * centred, axis=-1, keepdims=True))
    return centred * lax.rsqrt(spread + epsilon) * gain

def mlp_partial(pages, dw_weight, dw_bias, norm1_gain, fc1_w, fc1_b, fc2_w):
    convolved = depthwise(pages, dw_weight, dw_bias)
    flattened = convolved.reshape(-1, convolved.shape[-1])
    normed = layer_norm(flattened, norm1_gain, 1e-06).astype(jnp.bfloat16)
    hidden = jax.nn.gelu(jnp.dot(normed, fc1_w, preferred_element_type=jnp.float32) + fc1_b, approximate=False).astype(jnp.bfloat16)
    return jnp.dot(hidden, fc2_w, preferred_element_type=jnp.float32)

def reference(pages, valid_counts, dw_weight, dw_bias, norm1_gain, fc1_w, fc1_b, fc2_w, fc2_b, layer_scale, norm2_gain, w_query, w_key, w_value, w_out):
    channels = pages.shape[-1]
    partial_sum = mlp_partial(pages, dw_weight, dw_bias, norm1_gain, fc1_w, fc1_b, fc2_w)
    block = pages.reshape(-1, channels).astype(jnp.float32) + layer_scale * (partial_sum + fc2_b)
    normed = layer_norm(block, norm2_gain, 1e-05).astype(jnp.bfloat16)
    tokens = normed.shape[0]
    queries = jnp.dot(normed, w_query, preferred_element_type=jnp.float32).astype(jnp.bfloat16)
    keys = jnp.dot(normed, w_key, preferred_element_type=jnp.float32).astype(jnp.bfloat16)
    values = jnp.dot(normed, w_value, preferred_element_type=jnp.float32).astype(jnp.bfloat16)
    queries = queries.reshape(tokens, HEADS, HD).transpose(1, 0, 2)
    keys = keys.reshape(tokens, KV_HEADS, HD).transpose(1, 0, 2)
    values = values.reshape(tokens, KV_HEADS, HD).transpose(1, 0, 2)
    page_tokens = GH * GW
    position = jnp.arange(tokens, dtype=jnp.int32)
    valid = position % page_tokens < valid_counts[position // page_tokens]
    group = HEADS // KV_HEADS
    scale = HD ** (-0.5)

    def one_head(head_index):
        query_head = queries[head_index]
        key_head = keys[head_index // group]
        value_head = values[head_index // group]
        scores = jnp.dot(query_head, key_head.T, preferred_element_type=jnp.float32) * scale
        scores = jnp.where(valid[None, :], scores, -1e+30)
        row_top = lax.optimization_barrier(jnp.max(scores, axis=1, keepdims=True))
        exponent = jnp.where(valid[None, :], jnp.exp(scores - row_top), 0.0)
        denominator = lax.optimization_barrier(jnp.sum(exponent, axis=1, keepdims=True))
        weighted = jnp.dot(exponent.astype(jnp.bfloat16), value_head, preferred_element_type=jnp.float32)
        return (weighted / denominator).astype(jnp.bfloat16)
    attended = lax.map(one_head, jnp.arange(HEADS, dtype=jnp.int32))
    attended = attended.transpose(1, 0, 2).reshape(tokens, HEADS * HD)
    return jnp.dot(attended, w_out, preferred_element_type=jnp.float32).astype(jnp.bfloat16)
```

```python
import functools

import jax
import jax.numpy as jnp
from jax import lax
from jax.experimental import pallas as pl
from jax.experimental.pallas import tpu as pltpu
from jax.sharding import PartitionSpec as P

HEADS = 32
KV_HEADS = 8
HD = 128
LOG2E = 1.4426950408889634
NEG = -1e30
BF = jnp.bfloat16
F32 = jnp.float32


def vmem_spec():
    return pl.BlockSpec(memory_space=pltpu.VMEM)


def smem_spec():
    return pl.BlockSpec(memory_space=pltpu.SMEM)


def normalise(values, gain, epsilon):
    centred = values - jnp.mean(values, axis=-1, keepdims=True)
    spread = jnp.mean(centred * centred, axis=-1, keepdims=True)
    return centred * lax.rsqrt(spread + epsilon) * gain


def mlp_kernel(pages, dw, dwb, gain, w1, b1, w2, out, padded, conv):
    height, breadth, channels = pages.shape
    padded[...] = jnp.zeros(padded.shape, F32)
    padded[3 : 3 + height, 8 : 8 + breadth, :] = pages[...].astype(F32)
    half = height // 2
    for start in range(0, channels, 128):
        lanes = slice(start, start + 128)
        for top in range(0, height, half):
            total = jnp.broadcast_to(dwb[0:1, lanes][None], (half, breadth, 128))
            for sideways in range(7):
                window = padded[top : top + half + 6, 5 + sideways : 5 + sideways + breadth, lanes]
                for vertical in range(7):
                    tap = dw[vertical, sideways : sideways + 1, lanes]
                    total = total + window[vertical : vertical + half] * tap[None]
            conv[top * breadth : (top + half) * breadth, lanes] = total.reshape(half * breadth, 128)
    normed = normalise(conv[...], gain[...], 1e-06).astype(BF)
    pre = jnp.dot(normed, w1[...], preferred_element_type=F32) + b1[...]
    hidden = (0.5 * pre * (1.0 + lax.erf(pre * 0.7071067811865476))).astype(BF)
    out[...] = jnp.dot(hidden, w2[...], preferred_element_type=F32).astype(BF)


def mlp(pages, dw, dwb, gain, w1, b1, w2):
    _, height, breadth, channels = pages.shape
    rows = height * breadth
    return pl.pallas_call(
        mlp_kernel,
        out_shape=jax.ShapeDtypeStruct((rows, channels), BF),
        in_specs=[vmem_spec()] * 7,
        out_specs=vmem_spec(),
        scratch_shapes=[
            pltpu.VMEM((height + 6, breadth + 16, channels), F32),
            pltpu.VMEM((rows, channels), F32),
        ],
        name="conv_mlp",
    )(pages[0], dw, dwb[None], gain[None], w1, b1[None], w2)


def block_kernel(place, parts, pages, scale, b2, gain, out):
    count, chunk, _ = parts.shape
    total = parts[0].astype(F32)
    for part in range(1, count):
        total = total + parts[part].astype(F32)
    start = pl.multiple_of(place[0] * chunk, chunk)
    own = pages[pl.ds(start, chunk), :].astype(F32)
    block = own + scale[...] * (total + b2[...])
    normed = normalise(block, gain[...], 1e-05).astype(BF)
    for part in range(count):
        out[part] = normed


def block_norm(place, parts, pages, scale, b2, gain):
    return pl.pallas_call(
        block_kernel,
        out_shape=jax.ShapeDtypeStruct(parts.shape, BF),
        in_specs=[smem_spec()] + [vmem_spec()] * 5,
        out_specs=vmem_spec(),
        name="block_norm",
    )(place, parts, pages, scale[None], b2[None], gain[None])


def kv_kernel(normed, wk, wv, out):
    tokens = normed[...]
    out[0, :, 0:HD] = jnp.dot(tokens, wv[...], preferred_element_type=F32).astype(BF)
    out[0, :, HD : 2 * HD] = jnp.dot(tokens, wk[...], preferred_element_type=F32).astype(BF)


def key_values(normed, wk, wv):
    rows = normed.shape[0]
    return pl.pallas_call(
        kv_kernel,
        out_shape=jax.ShapeDtypeStruct((1, rows, 2 * HD), BF),
        in_specs=[vmem_spec()] * 3,
        out_specs=vmem_spec(),
        name="key_values",
    )(normed, wk, wv)


def query_kernel(normed, wq, out):
    product = jnp.dot(normed[...], wq[...], preferred_element_type=F32) * (HD**-0.5 * LOG2E)
    for head in range(out.shape[0]):
        out[head] = product[:, head * HD : (head + 1) * HD].astype(BF)


def queries_of(normed, wq):
    rows = normed.shape[0]
    return pl.pallas_call(
        query_kernel,
        out_shape=jax.ShapeDtypeStruct((wq.shape[1] // HD, rows, HD), BF),
        in_specs=[vmem_spec()] * 2,
        out_specs=vmem_spec(),
        name="queries",
    )(normed, wq)


def attend_kernel(first, last, offset, sizes, *refs):
    refs = list(refs)
    counts = refs.pop(0)
    query = refs.pop(0)
    chunks = [refs.pop(0) for _ in sizes]
    if not first:
        top_in, sums_in = refs.pop(0), refs.pop(0)
    if last:
        w_out = refs.pop(0)
        mixed = refs.pop(0)
        top_out, sums_out = refs.pop(0), refs.pop(0)
    else:
        top_out, sums_out = refs.pop(0), refs.pop(0)
    heads, rows, _ = query.shape
    pages = []
    for chunk, size in zip(chunks, sizes):
        for index in range(size):
            pages.append((chunk, index, offset + len(pages)))
    tokens = chunks[0].shape[1]
    lane = lax.broadcasted_iota(jnp.int32, (1, tokens), 1)
    lane_kv = lax.broadcasted_iota(jnp.int32, (tokens, 2 * HD), 1)
    fresh = first
    for begin in range(0, len(pages), 4):
        group = pages[begin : begin + 4]
        keys, values, masks = [], [], []
        for chunk, index, number in group:
            both = chunk[index]
            keys.append(both[:, HD : 2 * HD])
            values.append(jnp.where(lane_kv < HD, both, jnp.ones_like(both)))
            masks.append(jnp.where(lane < counts[number], 0.0, NEG).astype(F32))
        for head in range(heads):
            scores = [
                lax.dot_general(query[head], key, (((1,), (1,)), ((), ())), preferred_element_type=F32) + mask
                for key, mask in zip(keys, masks)
            ]
            largest = functools.reduce(jnp.maximum, scores)
            top = jnp.max(largest, axis=1, keepdims=True)
            if not fresh:
                source_top, source_sums = (top_in, sums_in) if begin == 0 else (top_out, sums_out)
                before = source_top[head][:, 0:1]
                top = jnp.maximum(top, before)
                carried = source_sums[head] * jnp.exp2(before - top)
            total = functools.reduce(
                jnp.add,
                [
                    jnp.dot(jnp.exp2(score - top).astype(BF), value, preferred_element_type=F32)
                    for score, value in zip(scores, values)
                ],
            )
            if not fresh:
                total = total + carried
            sums_out[head] = total
            top_out[head] = jnp.broadcast_to(top, (rows, HD))
        fresh = False
    if last:
        attended = jnp.concatenate(
            [(sums_out[head][:, 0:HD] / sums_out[head][:, HD : 2 * HD]).astype(BF) for head in range(heads)], axis=1
        )
        mixed[...] = jnp.dot(attended, w_out[...], preferred_element_type=F32).astype(BF)


def attend(counts, query, chunks, offset, carry=None, w_out=None):
    heads, rows, _ = query.shape
    sizes = tuple(chunk.shape[0] for chunk in chunks)
    state = [jax.ShapeDtypeStruct((heads, rows, HD), F32), jax.ShapeDtypeStruct((heads, rows, 2 * HD), F32)]
    operands = [counts, query, *chunks]
    if carry is not None:
        operands += list(carry)
    scratch = []
    if w_out is not None:
        operands.append(w_out)
        out_shape = [jax.ShapeDtypeStruct((rows, w_out.shape[1]), BF)]
        scratch = [pltpu.VMEM(one.shape, F32) for one in state]
    else:
        out_shape = state
    pairs = sum(sizes) * chunks[0].shape[1] * heads * rows
    return pl.pallas_call(
        functools.partial(attend_kernel, carry is None, w_out is not None, offset, sizes),
        out_shape=out_shape,
        in_specs=[smem_spec()] + [vmem_spec()] * (len(operands) - 1),
        out_specs=[vmem_spec()] * len(out_shape),
        scratch_shapes=scratch,
        cost_estimate=pl.CostEstimate(flops=pairs * 512, transcendentals=pairs, bytes_accessed=4 * 2**20),
        name="attend",
    )(*operands)


def total_kernel(parts, out):
    total = parts[0].astype(F32)
    for part in range(1, parts.shape[0]):
        total = total + parts[part].astype(F32)
    out[...] = total.astype(BF)


def total_of(parts):
    return pl.pallas_call(
        total_kernel,
        out_shape=jax.ShapeDtypeStruct(parts.shape[1:], BF),
        in_specs=[vmem_spec()],
        out_specs=vmem_spec(),
        name="total",
    )(parts)


def per_device(
    pages,
    valid_counts,
    dw_weight,
    dw_bias,
    norm1_gain,
    fc1_w,
    fc1_b,
    fc2_w,
    fc2_b,
    layer_scale,
    norm2_gain,
    w_query,
    w_key,
    w_value,
    w_out,
):
    channels = pages.shape[-1]
    rows = pages.shape[1] * pages.shape[2]
    groups = lax.axis_size("head")
    blocks = lax.axis_size("blk")
    depth = blocks // 4
    share = rows // groups

    def flip_y(array):
        return lax.ppermute(array, "blk", [(i, (i + 2 * depth) % blocks) for i in range(blocks)])

    def flip_core(array):
        return lax.ppermute(array, "blk", [(i, i ^ 1) for i in range(blocks)])

    def along_z(array, step):
        def target(i):
            return i // (2 * depth) * (2 * depth) + (i + 2 * step) % (2 * depth)

        return lax.ppermute(array, "blk", [(i, target(i)) for i in range(blocks)])

    own = lax.axis_index("blk").astype(jnp.int32)
    base_y, base_z, base_core = own // (2 * depth), own // 2 % depth, own % 2

    order = []
    for shifts in ((0,), (-1, 1), (-2, 2), (-3, 3), (4,)):
        for core in (0, 1):
            for side in (0, 1):
                for shift in shifts:
                    order.append((side, shift, core))
    sides = jnp.array([one[0] for one in order], jnp.int32)
    shifts = jnp.array([one[1] for one in order], jnp.int32)
    cores = jnp.array([one[2] for one in order], jnp.int32)
    numbers = (base_y ^ sides) * (2 * depth) + (base_z + shifts) % depth * 2 + (base_core ^ cores)
    counts = valid_counts[numbers]
    place = lax.axis_index("head").astype(jnp.int32)[None]

    partial = mlp(pages, dw_weight, dw_bias, norm1_gain, fc1_w, fc1_b, fc2_w)
    parts = lax.all_to_all(partial.reshape(groups, share, channels), "head", 0, 0, tiled=True)
    copies = block_norm(place, parts, pages.reshape(rows, channels), layer_scale, fc2_b, norm2_gain)
    normed = lax.all_to_all(copies, "head", 0, 0, tiled=True).reshape(rows, channels)

    start = key_values(normed, w_key, w_value)
    up, down = along_z(start, 1), along_z(start, -1)
    query = queries_of(normed, w_query)
    pair = jnp.concatenate([start, flip_y(start)])
    pair_core = flip_core(pair)

    def spread(array):
        both = jnp.concatenate([array, flip_y(array)])
        return both, flip_core(both)

    one = spread(jnp.concatenate([up, down]))
    up, down = along_z(up, 1), along_z(down, -1)
    two = spread(jnp.concatenate([up, down]))
    up, down = along_z(up, 1), along_z(down, -1)
    three = spread(jnp.concatenate([up, down]))
    up, down = along_z(up[:, : rows // 2], 1), along_z(down[:, rows // 2 :], -1)
    four = spread(jnp.concatenate([up, down], axis=1))

    carry = attend(counts, query, [pair, pair_core, *one], 0)
    carry = attend(counts, query, [*two], 12, carry)
    carry = attend(counts, query, [*three], 20, carry)
    (mixed,) = attend(counts, query, [*four], 28, carry, w_out)
    parts = lax.all_to_all(mixed.reshape(groups, share, channels), "head", 0, 0, tiled=True)
    return total_of(parts)


def solution(mesh):
    in_specs = (
        P("blk", None, None, None),
        P(),
        P(),
        P(),
        P(),
        P(None, "head"),
        P("head"),
        P("head", None),
        P(),
        P(),
        P(),
        P(None, "head"),
        P(None, "head"),
        P(None, "head"),
        P("head", None),
    )
    out_specs = P(("blk", "head"), None)
    return jax.shard_map(per_device, mesh=mesh, in_specs=in_specs, out_specs=out_specs, check_vma=False)
```

```python
import functools

import jax
import jax.numpy as jnp
from jax import lax
from jax.experimental import pallas as pl
from jax.experimental.pallas import tpu as pltpu
from jax.sharding import PartitionSpec as P

HEADS = 32
KV_HEADS = 8
HD = 128
LANES = 128
LOG2E = 1.4426950408889634
NEG = -1e30
BF = jnp.bfloat16
F32 = jnp.float32


def params(mebibytes):
    return pltpu.CompilerParams(vmem_limit_bytes=mebibytes * 2**20)


def vmem_spec():
    return pl.BlockSpec(memory_space=pltpu.VMEM)


def smem_spec():
    return pl.BlockSpec(memory_space=pltpu.SMEM)


def fold_lanes(pieces):
    return jnp.sum(functools.reduce(jnp.add, pieces), axis=-1, keepdims=True)


def normalise(pieces, gain, epsilon):
    width = len(pieces) * pieces[0].shape[-1]
    mean = fold_lanes(pieces) / width
    centred = [piece - mean for piece in pieces]
    spread = fold_lanes([piece * piece for piece in centred]) / width
    factor = lax.rsqrt(spread + epsilon)
    return [(piece * factor * gain[index : index + 1, :]).astype(BF) for index, piece in enumerate(centred)]


def lane_rows(vector):
    return vector.reshape(-1, LANES)


def mlp_kernel(pages, dw, dwb, gain, w1_hbm, b1, w2_hbm, out, padded, conv, w1, w2, arrived):
    loads = [
        pltpu.make_async_copy(w1_hbm, w1, arrived.at[0]),
        pltpu.make_async_copy(w2_hbm, w2, arrived.at[1]),
    ]
    for load in loads:
        load.start()
    height, breadth, channels = pages.shape
    half = height // 2
    column = lax.broadcasted_iota(jnp.int32, (half, breadth, LANES), 1)
    blank = jnp.zeros((3, breadth, LANES), F32)
    for chunk in range(channels // LANES):
        lanes = slice(chunk * LANES, (chunk + 1) * LANES)
        padded[chunk, 0:3] = blank
        padded[chunk, 3 + height : 6 + height] = blank
        padded[chunk, 3 : 3 + height] = pages[:, :, lanes].astype(F32)
        for top in range(0, height, half):
            total = jnp.broadcast_to(dwb[chunk : chunk + 1, :][None], (half, breadth, LANES))
            for sideways in range(7):
                product = None
                for vertical in range(7):
                    tap = dw[vertical, sideways : sideways + 1, lanes][None]
                    term = padded[chunk, top + vertical : top + vertical + half] * tap
                    product = term if product is None else product + term
                offset = sideways - 3
                if offset:
                    rolled = pltpu.roll(product, (-offset) % breadth, axis=1)
                    inside = (column + offset >= 0) if offset < 0 else (column + offset < breadth)
                    product = jnp.where(inside, rolled, 0.0)
                total = total + product
            conv[chunk, top * breadth : (top + half) * breadth] = total.reshape(half * breadth, LANES)
    normed = normalise([conv[chunk] for chunk in range(channels // LANES)], gain, 1e-06)
    loads[0].wait()
    product = jnp.dot(jnp.concatenate(normed, axis=1), w1[...], preferred_element_type=F32)
    hidden = []
    for chunk in range(product.shape[1] // LANES):
        pre = product[:, chunk * LANES : (chunk + 1) * LANES] + b1[chunk : chunk + 1, :]
        hidden.append((0.5 * pre * (1.0 + lax.erf(pre * 0.7071067811865476))).astype(BF))
    loads[1].wait()
    out[...] = jnp.dot(jnp.concatenate(hidden, axis=1), w2[...], preferred_element_type=F32).astype(BF)


def mlp(pages, dw, dwb, gain, w1, b1, w2):
    _, height, breadth, channels = pages.shape
    rows = height * breadth
    hbm = pl.BlockSpec(memory_space=pltpu.HBM)
    return pl.pallas_call(
        mlp_kernel,
        out_shape=jax.ShapeDtypeStruct((rows, channels), BF),
        in_specs=[vmem_spec()] * 4 + [hbm, vmem_spec(), hbm],
        out_specs=vmem_spec(),
        scratch_shapes=[
            pltpu.VMEM((channels // LANES, height + 6, breadth, LANES), F32),
            pltpu.VMEM((channels // LANES, rows, LANES), F32),
            pltpu.VMEM(w1.shape, w1.dtype),
            pltpu.VMEM(w2.shape, w2.dtype),
            pltpu.SemaphoreType.DMA((2,)),
        ],
        compiler_params=params(16),
        name="conv_mlp",
    )(pages[0], dw, lane_rows(dwb), lane_rows(gain), w1, lane_rows(b1), w2)


def block_kernel(place, parts, pages, scale, b2, gain, out):
    count, chunk, channels = parts.shape
    start = pl.multiple_of(place[0] * chunk, chunk)
    block = []
    for index in range(channels // LANES):
        lanes = slice(index * LANES, (index + 1) * LANES)
        row = slice(index, index + 1)
        total = functools.reduce(jnp.add, [parts[part, :, lanes].astype(F32) for part in range(count)])
        own = pages[pl.ds(start, chunk), lanes].astype(F32)
        block.append(own + scale[row, :] * (total + b2[row, :]))
    normed = jnp.concatenate(normalise(block, gain, 1e-05), axis=1)
    for part in range(count):
        out[part] = normed


def block_norm(place, parts, pages, scale, b2, gain):
    return pl.pallas_call(
        block_kernel,
        out_shape=jax.ShapeDtypeStruct(parts.shape, BF),
        in_specs=[smem_spec()] + [vmem_spec()] * 5,
        out_specs=vmem_spec(),
        compiler_params=params(8),
        name="block_norm",
    )(place, parts, pages, lane_rows(scale), lane_rows(b2), lane_rows(gain))


def kv_kernel(normed, wk, wv, out):
    tokens = normed[...]
    out[0, :, 0:HD] = jnp.dot(tokens, wv[...], preferred_element_type=F32).astype(BF)
    out[0, :, HD : 2 * HD] = jnp.dot(tokens, wk[...], preferred_element_type=F32).astype(BF)


def key_values(normed, wk, wv):
    rows = normed.shape[0]
    return pl.pallas_call(
        kv_kernel,
        out_shape=jax.ShapeDtypeStruct((1, rows, 2 * HD), BF),
        in_specs=[vmem_spec()] * 3,
        out_specs=vmem_spec(),
        compiler_params=params(8),
        name="key_values",
    )(normed, wk, wv)


def query_kernel(normed, wq, out):
    product = jnp.dot(normed[...], wq[...], preferred_element_type=F32) * (HD**-0.5 * LOG2E)
    for head in range(out.shape[0]):
        out[head] = product[:, head * HD : (head + 1) * HD].astype(BF)


def queries_of(normed, wq):
    rows = normed.shape[0]
    return pl.pallas_call(
        query_kernel,
        out_shape=jax.ShapeDtypeStruct((wq.shape[1] // HD, rows, HD), BF),
        in_specs=[vmem_spec()] * 2,
        out_specs=vmem_spec(),
        compiler_params=params(8),
        name="queries",
    )(normed, wq)


def attend_kernel(first, last, places, depth, sizes, *refs):
    refs = list(refs)
    valid_counts, own = refs.pop(0), refs.pop(0)
    query = refs.pop(0)
    chunks = [refs.pop(0) for _ in sizes]
    if not first:
        top_in, sums_in = refs.pop(0), refs.pop(0)
    if last:
        w_out = refs.pop(0)
        mixed = refs.pop(0)
        top_out, sums_out = refs.pop(0), refs.pop(0)
    else:
        top_out, sums_out = refs.pop(0), refs.pop(0)
    heads, rows, _ = query.shape
    here = own[0]
    here_y, here_z, here_core = lax.div(here, 2 * depth), lax.rem(lax.div(here, 2), depth), lax.rem(here, 2)
    pages = []
    for chunk, size in zip(chunks, sizes):
        for index in range(size):
            side, shift, core = places[len(pages)]
            number = (here_y ^ side) * (2 * depth) + lax.rem(here_z + shift % depth, depth) * 2 + (here_core ^ core)
            pages.append((chunk, index, valid_counts[number]))
    group_size = 4 if len(pages) % 4 == 0 else min(3, len(pages))
    tokens = chunks[0].shape[1]
    lane = lax.broadcasted_iota(jnp.int32, (1, tokens), 1)
    lane_kv = lax.broadcasted_iota(jnp.int32, (tokens, 2 * HD), 1)
    fresh = first
    for begin in range(0, len(pages), group_size):
        group = pages[begin : begin + group_size]
        keys, values, masks = [], [], []
        for chunk, index, count in group:
            both = chunk[index]
            keys.append(both[:, HD : 2 * HD])
            values.append(jnp.where(lane_kv < HD, both, jnp.ones_like(both)))
            masks.append(jnp.where(lane < count, 0.0, NEG).astype(F32))
        for head in range(heads):
            scores = [
                lax.dot_general(query[head], key, (((1,), (1,)), ((), ())), preferred_element_type=F32) + mask
                for key, mask in zip(keys, masks)
            ]
            largest = functools.reduce(jnp.maximum, scores)
            top = jnp.max(largest, axis=1, keepdims=True)
            if not fresh:
                source_top, source_sums = (top_in, sums_in) if begin == 0 else (top_out, sums_out)
                before = source_top[head][:, 0:1]
                top = jnp.maximum(top, before)
                carried = source_sums[head] * jnp.exp2(before - top)
            total = functools.reduce(
                jnp.add,
                [
                    jnp.dot(jnp.exp2(score - top).astype(BF), value, preferred_element_type=F32)
                    for score, value in zip(scores, values)
                ],
            )
            if not fresh:
                total = total + carried
            sums_out[head] = total
            top_out[head] = jnp.broadcast_to(top, (rows, HD))
        fresh = False
    if last:
        attended = jnp.concatenate(
            [(sums_out[head][:, 0:HD] / sums_out[head][:, HD : 2 * HD]).astype(BF) for head in range(heads)], axis=1
        )
        mixed[...] = jnp.dot(attended, w_out[...], preferred_element_type=F32).astype(BF)


def attend(valid_counts, own, depth, query, pieces, carry=None, w_out=None):
    heads, rows, _ = query.shape
    chunks = [piece[0] for piece in pieces]
    places = [place for piece in pieces for place in piece[1]]
    sizes = tuple(chunk.shape[0] for chunk in chunks)
    state = [jax.ShapeDtypeStruct((heads, rows, HD), F32), jax.ShapeDtypeStruct((heads, rows, 2 * HD), F32)]
    operands = [valid_counts, own, query, *chunks]
    if carry is not None:
        operands += list(carry)
    scratch = []
    if w_out is not None:
        operands.append(w_out)
        out_shape = [jax.ShapeDtypeStruct((rows, w_out.shape[1]), BF)]
        scratch = [pltpu.VMEM(one.shape, F32) for one in state]
    else:
        out_shape = state
    pairs = sum(sizes) * chunks[0].shape[1] * heads * rows
    return pl.pallas_call(
        functools.partial(attend_kernel, carry is None, w_out is not None, places, depth, sizes),
        out_shape=out_shape,
        in_specs=[smem_spec()] * 2 + [vmem_spec()] * (len(operands) - 2),
        out_specs=[vmem_spec()] * len(out_shape),
        scratch_shapes=scratch,
        cost_estimate=pl.CostEstimate(flops=pairs * 512, transcendentals=pairs, bytes_accessed=4 * 2**20),
        compiler_params=params(28),
        name="attend",
    )(*operands)


def total_kernel(parts, out):
    total = parts[0].astype(F32)
    for part in range(1, parts.shape[0]):
        total = total + parts[part].astype(F32)
    out[...] = total.astype(BF)


def total_of(parts):
    return pl.pallas_call(
        total_kernel,
        out_shape=jax.ShapeDtypeStruct(parts.shape[1:], BF),
        in_specs=[vmem_spec()],
        out_specs=vmem_spec(),
        compiler_params=params(8),
        name="total",
    )(parts)


def per_device(
    pages,
    valid_counts,
    dw_weight,
    dw_bias,
    norm1_gain,
    fc1_w,
    fc1_b,
    fc2_w,
    fc2_b,
    layer_scale,
    norm2_gain,
    w_query,
    w_key,
    w_value,
    w_out,
):
    channels = pages.shape[-1]
    rows = pages.shape[1] * pages.shape[2]
    groups = lax.axis_size("head")
    blocks = lax.axis_size("blk")
    depth = blocks // 4
    share = rows // groups

    def flip_y(array):
        return lax.ppermute(array, "blk", [(i, (i + 2 * depth) % blocks) for i in range(blocks)])

    def flip_core(array):
        return lax.ppermute(array, "blk", [(i, i ^ 1) for i in range(blocks)])

    def along_z(array, step):
        def target(i):
            return i // (2 * depth) * (2 * depth) + (i + 2 * step) % (2 * depth)

        return lax.ppermute(array, "blk", [(i, target(i)) for i in range(blocks)])

    own = lax.axis_index("blk").astype(jnp.int32)[None]
    place = lax.axis_index("head").astype(jnp.int32)[None]
    hold = lax.optimization_barrier

    partial = mlp(pages, dw_weight, dw_bias, norm1_gain, fc1_w, fc1_b, fc2_w)
    parts = lax.all_to_all(partial.reshape(groups, share, channels), "head", 0, 0, tiled=True)
    copies = block_norm(place, parts, pages.reshape(rows, channels), layer_scale, fc2_b, norm2_gain)
    normed = lax.all_to_all(copies, "head", 0, 0, tiled=True).reshape(rows, channels)

    def spots(shifts, sides, core):
        return [(side, shift, core) for side in sides for shift in shifts]

    def fold(pieces, carry=None, weight=None):
        return attend(valid_counts, own, depth, query, pieces, carry, weight)

    start = key_values(normed, w_key, w_value)
    up, down = along_z(start, 1), along_z(start, -1)
    other = flip_y(start)
    query = queries_of(normed, w_query)

    up, down, query = hold((up, down, query))
    near = jnp.concatenate([up, down])
    up, down = along_z(up, 1), along_z(down, -1)
    near_other = flip_y(near)
    crossed = flip_core(jnp.concatenate([start, other]))
    carry = fold([(start, spots((0,), (0,), 0)), (other, spots((0,), (1,), 0))])
    waiting = (crossed, spots((0,), (0, 1), 1))

    for hop in (1, 2, 3):
        up, down, carry = hold((up, down, carry))
        following = jnp.concatenate([up, down], axis=0 if hop < 3 else 1)
        if hop == 1:
            up, down = along_z(up, 1), along_z(down, -1)
        elif hop == 2:
            up, down = along_z(up[:, : rows // 2], 1), along_z(down[:, rows // 2 :], -1)
        following_other = flip_y(following)
        crossed = flip_core(jnp.concatenate([near, near_other]))
        shifts = (-hop, hop)
        carry = fold([waiting, (near, spots(shifts, (0,), 0)), (near_other, spots(shifts, (1,), 0))], carry)
        waiting = (crossed, spots(shifts, (0, 1), 1))
        near, near_other = following, following_other

    near_other, *carry = hold((near_other, *carry))
    crossed = flip_core(jnp.concatenate([near, near_other]))
    carry = fold([waiting, (near, spots((4,), (0,), 0)), (near_other, spots((4,), (1,), 0))], carry)
    (mixed,) = fold([(crossed, spots((4,), (0, 1), 1))], carry, w_out)
    parts = lax.all_to_all(mixed.reshape(groups, share, channels), "head", 0, 0, tiled=True)
    return total_of(parts)


def solution(mesh):
    in_specs = (
        P("blk", None, None, None),
        P(),
        P(),
        P(),
        P(),
        P(None, "head"),
        P("head"),
        P("head", None),
        P(),
        P(),
        P(),
        P(None, "head"),
        P(None, "head"),
        P(None, "head"),
        P("head", None),
    )
    out_specs = P(("blk", "head"), None)
    return jax.shard_map(per_device, mesh=mesh, in_specs=in_specs, out_specs=out_specs, check_vma=False)
```

```python
import functools

import jax
import jax.numpy as jnp
from jax import lax
from jax.experimental import pallas as pl
from jax.experimental.pallas import tpu as pltpu
from jax.sharding import PartitionSpec as P

HEADS = 32
KV_HEADS = 8
HD = 128
LANES = 128
LOG2E = 1.4426950408889634
NEG = -1e30
BF = jnp.bfloat16
F32 = jnp.float32


def params(mebibytes):
    return pltpu.CompilerParams(vmem_limit_bytes=mebibytes * 2**20)


def vmem_spec():
    return pl.BlockSpec(memory_space=pltpu.VMEM)


def smem_spec():
    return pl.BlockSpec(memory_space=pltpu.SMEM)


def fold_lanes(pieces):
    return jnp.sum(functools.reduce(jnp.add, pieces), axis=-1, keepdims=True)


def normalise(pieces, gain, epsilon):
    width = len(pieces) * pieces[0].shape[-1]
    mean = fold_lanes(pieces) / width
    centred = [piece - mean for piece in pieces]
    spread = fold_lanes([piece * piece for piece in centred]) / width
    factor = lax.rsqrt(spread + epsilon)
    return [(piece * factor * gain[index : index + 1, :]).astype(BF) for index, piece in enumerate(centred)]


def fixed(array):
    return pltpu.with_memory_space_constraint(array, pltpu.HBM)


def lane_rows(vector):
    return vector.reshape(-1, LANES)


def mlp_kernel(pages_hbm, dw_hbm, dwb_hbm, gain_hbm, w1_hbm, b1_hbm, w2_hbm, out, *scratch):
    padded, conv, pages, dw, dwb, gain, w1, b1, w2, arrived = scratch
    pairs = (
        (w1_hbm, w1),
        (w2_hbm, w2),
        (b1_hbm, b1),
        (gain_hbm, gain),
        (dwb_hbm, dwb),
        (dw_hbm, dw),
        (pages_hbm, pages),
    )
    loads = [pltpu.make_async_copy(source, target, arrived.at[index]) for index, (source, target) in enumerate(pairs)]
    for load in reversed(loads):
        load.start()
    for load in loads[2:]:
        load.wait()
    height, breadth, channels = pages.shape
    half = height // 2
    column = lax.broadcasted_iota(jnp.int32, (half, breadth, LANES), 1)
    blank = jnp.zeros((3, breadth, LANES), F32)
    for chunk in range(channels // LANES):
        lanes = slice(chunk * LANES, (chunk + 1) * LANES)
        padded[chunk, 0:3] = blank
        padded[chunk, 3 + height : 6 + height] = blank
        padded[chunk, 3 : 3 + height] = pages[:, :, lanes].astype(F32)
        for top in range(0, height, half):
            total = jnp.broadcast_to(dwb[chunk : chunk + 1, :][None], (half, breadth, LANES))
            for sideways in range(7):
                product = None
                for vertical in range(7):
                    tap = dw[vertical, sideways : sideways + 1, lanes][None]
                    term = padded[chunk, top + vertical : top + vertical + half] * tap
                    product = term if product is None else product + term
                offset = sideways - 3
                if offset:
                    rolled = pltpu.roll(product, (-offset) % breadth, axis=1)
                    inside = (column + offset >= 0) if offset < 0 else (column + offset < breadth)
                    product = jnp.where(inside, rolled, 0.0)
                total = total + product
            conv[chunk, top * breadth : (top + half) * breadth] = total.reshape(half * breadth, LANES)
    normed = normalise([conv[chunk] for chunk in range(channels // LANES)], gain, 1e-06)
    loads[0].wait()
    product = jnp.dot(jnp.concatenate(normed, axis=1), w1[...], preferred_element_type=F32)
    hidden = []
    for chunk in range(product.shape[1] // LANES):
        pre = product[:, chunk * LANES : (chunk + 1) * LANES] + b1[chunk : chunk + 1, :]
        hidden.append((0.5 * pre * (1.0 + lax.erf(pre * 0.7071067811865476))).astype(BF))
    loads[1].wait()
    out[...] = jnp.dot(jnp.concatenate(hidden, axis=1), w2[...], preferred_element_type=F32).astype(BF)


def mlp(pages, dw, dwb, gain, w1, b1, w2):
    _, height, breadth, channels = pages.shape
    rows = height * breadth
    operands = (pages[0], dw, lane_rows(dwb), lane_rows(gain), w1, lane_rows(b1), w2)
    return pl.pallas_call(
        mlp_kernel,
        out_shape=jax.ShapeDtypeStruct((rows, channels), BF),
        in_specs=[pl.BlockSpec(memory_space=pltpu.HBM)] * 7,
        out_specs=vmem_spec(),
        scratch_shapes=[
            pltpu.VMEM((channels // LANES, height + 6, breadth, LANES), F32),
            pltpu.VMEM((channels // LANES, rows, LANES), F32),
            *[pltpu.VMEM(operand.shape, operand.dtype) for operand in operands],
            pltpu.SemaphoreType.DMA((7,)),
        ],
        compiler_params=params(16),
        name="conv_mlp",
    )(*[fixed(operand) for operand in operands])


def block_kernel(place, parts, pages, scale, b2, gain, out):
    count, chunk, channels = parts.shape
    start = pl.multiple_of(place[0] * chunk, chunk)
    block = []
    for index in range(channels // LANES):
        lanes = slice(index * LANES, (index + 1) * LANES)
        row = slice(index, index + 1)
        total = functools.reduce(jnp.add, [parts[part, :, lanes].astype(F32) for part in range(count)])
        own = pages[pl.ds(start, chunk), lanes].astype(F32)
        block.append(own + scale[row, :] * (total + b2[row, :]))
    normed = jnp.concatenate(normalise(block, gain, 1e-05), axis=1)
    for part in range(count):
        out[part] = normed


def block_norm(place, parts, pages, scale, b2, gain):
    return pl.pallas_call(
        block_kernel,
        out_shape=jax.ShapeDtypeStruct(parts.shape, BF),
        in_specs=[smem_spec()] + [vmem_spec()] * 5,
        out_specs=vmem_spec(),
        compiler_params=params(8),
        name="block_norm",
    )(place, parts, pages, lane_rows(scale), lane_rows(b2), lane_rows(gain))


def kv_kernel(normed, wk, wv, out):
    tokens = normed[...]
    out[0, :, 0:HD] = jnp.dot(tokens, wv[...], preferred_element_type=F32).astype(BF)
    out[0, :, HD : 2 * HD] = jnp.dot(tokens, wk[...], preferred_element_type=F32).astype(BF)


def key_values(normed, wk, wv):
    rows = normed.shape[0]
    return pl.pallas_call(
        kv_kernel,
        out_shape=jax.ShapeDtypeStruct((1, rows, 2 * HD), BF),
        in_specs=[vmem_spec()] * 3,
        out_specs=vmem_spec(),
        compiler_params=params(8),
        name="key_values",
    )(normed, wk, wv)


def query_kernel(normed, wq, out):
    product = jnp.dot(normed[...], wq[...], preferred_element_type=F32) * (HD**-0.5 * LOG2E)
    for head in range(out.shape[0]):
        out[head] = product[:, head * HD : (head + 1) * HD].astype(BF)


def queries_of(normed, wq):
    rows = normed.shape[0]
    return pl.pallas_call(
        query_kernel,
        out_shape=jax.ShapeDtypeStruct((wq.shape[1] // HD, rows, HD), BF),
        in_specs=[vmem_spec()] * 2,
        out_specs=vmem_spec(),
        compiler_params=params(8),
        name="queries",
    )(normed, wq)


def attend_kernel(first, last, places, depth, sizes, *refs):
    refs = list(refs)
    valid_counts, own = refs.pop(0), refs.pop(0)
    query = refs.pop(0)
    chunks = [refs.pop(0) for _ in sizes]
    if not first:
        top_in, sums_in = refs.pop(0), refs.pop(0)
    if last:
        w_out = refs.pop(0)
        mixed = refs.pop(0)
        top_out, sums_out = refs.pop(0), refs.pop(0)
    else:
        top_out, sums_out = refs.pop(0), refs.pop(0)
    heads, rows, _ = query.shape
    here = own[0]
    here_y, here_z, here_core = lax.div(here, 2 * depth), lax.rem(lax.div(here, 2), depth), lax.rem(here, 2)
    pages = []
    for chunk, size in zip(chunks, sizes):
        for index in range(size):
            side, shift, core = places[len(pages)]
            number = (here_y ^ side) * (2 * depth) + lax.rem(here_z + shift % depth, depth) * 2 + (here_core ^ core)
            pages.append((chunk, index, valid_counts[number]))
    group_size = 4 if len(pages) in (4, 7, 8) else min(3, len(pages))
    tokens = chunks[0].shape[1]
    lane = lax.broadcasted_iota(jnp.int32, (1, tokens), 1)
    lane_kv = lax.broadcasted_iota(jnp.int32, (tokens, 2 * HD), 1)
    fresh = first
    for begin in range(0, len(pages), group_size):
        group = pages[begin : begin + group_size]
        keys, values, masks = [], [], []
        for chunk, index, count in group:
            both = chunk[index]
            keys.append(both[:, HD : 2 * HD])
            values.append(jnp.where(lane_kv < HD, both, jnp.ones_like(both)))
            masks.append(jnp.where(lane < count, 0.0, NEG).astype(F32))
        for head in range(heads):
            scores = [
                lax.dot_general(query[head], key, (((1,), (1,)), ((), ())), preferred_element_type=F32) + mask
                for key, mask in zip(keys, masks)
            ]
            largest = functools.reduce(jnp.maximum, scores)
            top = jnp.max(largest, axis=1, keepdims=True)
            if not fresh:
                source_top, source_sums = (top_in, sums_in) if begin == 0 else (top_out, sums_out)
                before = source_top[head][:, 0:1]
                top = jnp.maximum(top, before)
                carried = source_sums[head] * jnp.exp2(before - top)
            total = functools.reduce(
                jnp.add,
                [
                    jnp.dot(jnp.exp2(score - top).astype(BF), value, preferred_element_type=F32)
                    for score, value in zip(scores, values)
                ],
            )
            if not fresh:
                total = total + carried
            sums_out[head] = total
            top_out[head] = jnp.broadcast_to(top, (rows, HD))
        fresh = False
    if last:
        attended = jnp.concatenate(
            [(sums_out[head][:, 0:HD] / sums_out[head][:, HD : 2 * HD]).astype(BF) for head in range(heads)], axis=1
        )
        mixed[...] = jnp.dot(attended, w_out[...], preferred_element_type=F32).astype(BF)


def attend(valid_counts, own, depth, query, pieces, carry=None, w_out=None):
    heads, rows, _ = query.shape
    chunks = [piece[0] for piece in pieces]
    places = [place for piece in pieces for place in piece[1]]
    sizes = tuple(chunk.shape[0] for chunk in chunks)
    state = [jax.ShapeDtypeStruct((heads, rows, HD), F32), jax.ShapeDtypeStruct((heads, rows, 2 * HD), F32)]
    operands = [valid_counts, own, query, *chunks]
    if carry is not None:
        operands += list(carry)
    scratch = []
    if w_out is not None:
        operands.append(w_out)
        out_shape = [jax.ShapeDtypeStruct((rows, w_out.shape[1]), BF)]
        scratch = [pltpu.VMEM(one.shape, F32) for one in state]
    else:
        out_shape = state
    pairs = sum(sizes) * chunks[0].shape[1] * heads * rows
    return pl.pallas_call(
        functools.partial(attend_kernel, carry is None, w_out is not None, places, depth, sizes),
        out_shape=out_shape,
        in_specs=[smem_spec()] * 2 + [vmem_spec()] * (len(operands) - 2),
        out_specs=[vmem_spec()] * len(out_shape),
        scratch_shapes=scratch,
        cost_estimate=pl.CostEstimate(flops=pairs // 8, transcendentals=0, bytes_accessed=2**16),
        compiler_params=params(28),
        name="attend",
    )(*operands)


def total_kernel(parts, out):
    total = parts[0].astype(F32)
    for part in range(1, parts.shape[0]):
        total = total + parts[part].astype(F32)
    out[...] = total.astype(BF)


def total_of(parts):
    return pl.pallas_call(
        total_kernel,
        out_shape=jax.ShapeDtypeStruct(parts.shape[1:], BF),
        in_specs=[vmem_spec()],
        out_specs=vmem_spec(),
        compiler_params=params(8),
        name="total",
    )(parts)


def per_device(
    pages,
    valid_counts,
    dw_weight,
    dw_bias,
    norm1_gain,
    fc1_w,
    fc1_b,
    fc2_w,
    fc2_b,
    layer_scale,
    norm2_gain,
    w_query,
    w_key,
    w_value,
    w_out,
):
    channels = pages.shape[-1]
    rows = pages.shape[1] * pages.shape[2]
    groups = lax.axis_size("head")
    blocks = lax.axis_size("blk")
    depth = blocks // 4
    share = rows // groups

    def flip_y(array):
        return lax.ppermute(array, "blk", [(i, (i + 2 * depth) % blocks) for i in range(blocks)])

    def flip_core(array):
        return lax.ppermute(array, "blk", [(i, i ^ 1) for i in range(blocks)])

    def along_z(array, step):
        def target(i):
            return i // (2 * depth) * (2 * depth) + (i + 2 * step) % (2 * depth)

        return lax.ppermute(array, "blk", [(i, target(i)) for i in range(blocks)])

    def to_side(array, step):
        def target(i):
            turn = 2 * step if i // 2 % 2 == 0 else -2 * step
            return i // (2 * depth) * (2 * depth) + (i + turn) % (2 * depth)

        return lax.ppermute(array, "blk", [(i, target(i)) for i in range(blocks)])

    even = lax.axis_index("blk") // 2 % 2 == 0
    own = lax.axis_index("blk").astype(jnp.int32)[None]
    place = lax.axis_index("head").astype(jnp.int32)[None]
    hold = lax.optimization_barrier

    partial = mlp(pages, dw_weight, dw_bias, norm1_gain, fc1_w, fc1_b, fc2_w)
    parts = lax.all_to_all(partial.reshape(groups, share, channels), "head", 0, 0, tiled=True)
    copies = block_norm(place, parts, pages.reshape(rows, channels), layer_scale, fc2_b, norm2_gain)
    normed = lax.all_to_all(copies, "head", 0, 0, tiled=True).reshape(rows, channels)

    def spots(shifts, sides, core):
        return [(side, shift, core) for side in sides for shift in shifts]

    def fold(pieces, carry=None, weight=None):
        return attend(valid_counts, own, depth, query, pieces, carry, weight)

    start = key_values(normed, w_key, w_value)
    up, down = along_z(start, 1), along_z(start, -1)
    other = flip_y(start)
    query = queries_of(normed, w_query)
    carry = fold([(start, spots((0,), (0,), 0))])
    up, down, other, carry = hold((up, down, other, carry))

    near = jnp.concatenate([up, down])
    up, down = along_z(up, 1), along_z(down, -1)
    near_other = flip_y(near)
    crossed = flip_core(jnp.concatenate([start, other]))
    carry = fold([(other, spots((0,), (1,), 0)), (near, spots((-1, 1), (0,), 0))], carry)
    up, down, near_other, crossed, carry = hold((up, down, near_other, crossed, carry))
    waiting = (crossed, spots((0,), (0, 1), 1))

    second = jnp.concatenate([up, down])
    up, down = along_z(up, 1), along_z(down, -1)
    second_other = flip_y(second)
    crossed = flip_core(jnp.concatenate([near, near_other]))
    carry = fold([waiting, (near_other, spots((-1, 1), (1,), 0)), (second, spots((-2, 2), (0,), 0))], carry)
    up, down, second_other, crossed, carry = hold((up, down, second_other, crossed, carry))
    waiting = (crossed, spots((-1, 1), (0, 1), 1))

    third = jnp.concatenate([up, down])
    third_other = flip_y(third)
    far = to_side(jnp.where(even, up, down), 1)
    far_other = to_side(jnp.where(even, second_other[0:1], second_other[1:2]), 2)
    crossed = flip_core(jnp.concatenate([second, second_other]))
    carry = fold([waiting, (second_other, spots((-2, 2), (1,), 0))], carry)
    crossed, carry = hold((crossed, carry))
    waiting = (crossed, spots((-2, 2), (0, 1), 1))
    carry = fold([(third, spots((-3, 3), (0,), 0)), waiting], carry)
    third_other, far, far_other, carry = hold((third_other, far, far_other, carry))

    crossed = flip_core(jnp.concatenate([third, third_other, far, far_other]))
    carry = fold(
        [(third_other, spots((-3, 3), (1,), 0)), (far, spots((4,), (0,), 0)), (far_other, spots((4,), (1,), 0))], carry
    )
    crossed, carry = hold((crossed, carry))
    waiting = (crossed, spots((-3, 3), (0, 1), 1) + spots((4,), (0, 1), 1))
    (mixed,) = fold([waiting], carry, w_out)
    parts = lax.all_to_all(mixed.reshape(groups, share, channels), "head", 0, 0, tiled=True)
    return total_of(parts)


def solution(mesh):
    in_specs = (
        P("blk", None, None, None),
        P(),
        P(),
        P(),
        P(),
        P(None, "head"),
        P("head"),
        P("head", None),
        P(),
        P(),
        P(),
        P(None, "head"),
        P(None, "head"),
        P(None, "head"),
        P("head", None),
    )
    out_specs = P(("blk", "head"), None)
    return jax.shard_map(per_device, mesh=mesh, in_specs=in_specs, out_specs=out_specs, check_vma=False)
```

```python
import functools

import jax
import jax.numpy as jnp
from jax import lax
from jax.experimental import pallas as pl
from jax.experimental.pallas import tpu as pltpu
from jax.sharding import PartitionSpec as P

HEADS = 32
KV_HEADS = 8
HD = 128
LANES = 128
LOG2E = 1.4426950408889634
NEG = -1e30
BF = jnp.bfloat16
F32 = jnp.float32


def params(mebibytes):
    return pltpu.CompilerParams(vmem_limit_bytes=mebibytes * 2**20)


def vmem_spec():
    return pl.BlockSpec(memory_space=pltpu.VMEM)


def smem_spec():
    return pl.BlockSpec(memory_space=pltpu.SMEM)


def fold_lanes(pieces):
    return jnp.sum(functools.reduce(jnp.add, pieces), axis=-1, keepdims=True)


def normalise(pieces, gain, epsilon):
    width = len(pieces) * pieces[0].shape[-1]
    mean = fold_lanes(pieces) / width
    centred = [piece - mean for piece in pieces]
    spread = fold_lanes([piece * piece for piece in centred]) / width
    factor = lax.rsqrt(spread + epsilon)
    return [(piece * factor * gain[index : index + 1, :]).astype(BF) for index, piece in enumerate(centred)]


def fixed(array):
    return pltpu.with_memory_space_constraint(array, pltpu.HBM)


def lane_rows(vector):
    return vector.reshape(-1, LANES)


def mlp_kernel(pages_hbm, dw_hbm, dwb_hbm, gain_hbm, w1_hbm, b1_hbm, w2_hbm, out, *scratch):
    padded, conv, pages, dw, dwb, gain, w1, b1, w2, arrived = scratch
    pairs = (
        (w1_hbm, w1),
        (w2_hbm, w2),
        (b1_hbm, b1),
        (gain_hbm, gain),
        (dwb_hbm, dwb),
        (dw_hbm, dw),
        (pages_hbm, pages),
    )
    loads = [pltpu.make_async_copy(source, target, arrived.at[index]) for index, (source, target) in enumerate(pairs)]
    for load in reversed(loads):
        load.start()
    for load in loads[2:]:
        load.wait()
    height, breadth, channels = pages.shape
    half = height // 2
    column = lax.broadcasted_iota(jnp.int32, (half, breadth, LANES), 1)
    blank = jnp.zeros((3, breadth, LANES), F32)
    for chunk in range(channels // LANES):
        lanes = slice(chunk * LANES, (chunk + 1) * LANES)
        padded[chunk, 0:3] = blank
        padded[chunk, 3 + height : 6 + height] = blank
        padded[chunk, 3 : 3 + height] = pages[:, :, lanes].astype(F32)
        for top in range(0, height, half):
            total = jnp.broadcast_to(dwb[chunk : chunk + 1, :][None], (half, breadth, LANES))
            for sideways in range(7):
                product = None
                for vertical in range(7):
                    tap = dw[vertical, sideways : sideways + 1, lanes][None]
                    term = padded[chunk, top + vertical : top + vertical + half] * tap
                    product = term if product is None else product + term
                offset = sideways - 3
                if offset:
                    rolled = pltpu.roll(product, (-offset) % breadth, axis=1)
                    inside = (column + offset >= 0) if offset < 0 else (column + offset < breadth)
                    product = jnp.where(inside, rolled, 0.0)
                total = total + product
            conv[chunk, top * breadth : (top + half) * breadth] = total.reshape(half * breadth, LANES)
    normed = normalise([conv[chunk] for chunk in range(channels // LANES)], gain, 1e-06)
    loads[0].wait()
    product = jnp.dot(jnp.concatenate(normed, axis=1), w1[...], preferred_element_type=F32)
    hidden = []
    for chunk in range(product.shape[1] // LANES):
        pre = product[:, chunk * LANES : (chunk + 1) * LANES] + b1[chunk : chunk + 1, :]
        hidden.append((0.5 * pre * (1.0 + lax.erf(pre * 0.7071067811865476))).astype(BF))
    loads[1].wait()
    out[...] = jnp.dot(jnp.concatenate(hidden, axis=1), w2[...], preferred_element_type=F32).astype(BF)


def mlp(pages, dw, dwb, gain, w1, b1, w2):
    _, height, breadth, channels = pages.shape
    rows = height * breadth
    operands = (pages[0], dw, lane_rows(dwb), lane_rows(gain), w1, lane_rows(b1), w2)
    return pl.pallas_call(
        mlp_kernel,
        out_shape=jax.ShapeDtypeStruct((rows, channels), BF),
        in_specs=[pl.BlockSpec(memory_space=pltpu.HBM)] * 7,
        out_specs=vmem_spec(),
        scratch_shapes=[
            pltpu.VMEM((channels // LANES, height + 6, breadth, LANES), F32),
            pltpu.VMEM((channels // LANES, rows, LANES), F32),
            *[pltpu.VMEM(operand.shape, operand.dtype) for operand in operands],
            pltpu.SemaphoreType.DMA((7,)),
        ],
        compiler_params=params(16),
        name="conv_mlp",
    )(*[fixed(operand) for operand in operands])


def block_kernel(place, parts, pages, scale, b2, gain, out):
    count, chunk, channels = parts.shape
    start = pl.multiple_of(place[0] * chunk, chunk)
    block = []
    for index in range(channels // LANES):
        lanes = slice(index * LANES, (index + 1) * LANES)
        row = slice(index, index + 1)
        total = functools.reduce(jnp.add, [parts[part, :, lanes].astype(F32) for part in range(count)])
        own = pages[pl.ds(start, chunk), lanes].astype(F32)
        block.append(own + scale[row, :] * (total + b2[row, :]))
    normed = jnp.concatenate(normalise(block, gain, 1e-05), axis=1)
    for part in range(count):
        out[part] = normed


def block_norm(place, parts, pages, scale, b2, gain):
    return pl.pallas_call(
        block_kernel,
        out_shape=jax.ShapeDtypeStruct(parts.shape, BF),
        in_specs=[smem_spec()] + [vmem_spec()] * 5,
        out_specs=vmem_spec(),
        compiler_params=params(8),
        name="block_norm",
    )(place, parts, pages, lane_rows(scale), lane_rows(b2), lane_rows(gain))


def kv_kernel(normed, wk, wv, out):
    tokens = normed[...]
    out[0, :, 0:HD] = jnp.dot(tokens, wv[...], preferred_element_type=F32).astype(BF)
    out[0, :, HD : 2 * HD] = jnp.dot(tokens, wk[...], preferred_element_type=F32).astype(BF)


def key_values(normed, wk, wv):
    rows = normed.shape[0]
    return pl.pallas_call(
        kv_kernel,
        out_shape=jax.ShapeDtypeStruct((1, rows, 2 * HD), BF),
        in_specs=[vmem_spec()] * 3,
        out_specs=vmem_spec(),
        compiler_params=params(8),
        name="key_values",
    )(normed, wk, wv)


def query_kernel(normed, wq, out):
    product = jnp.dot(normed[...], wq[...], preferred_element_type=F32) * (HD**-0.5 * LOG2E)
    for head in range(out.shape[0]):
        out[head] = product[:, head * HD : (head + 1) * HD].astype(BF)


def queries_of(normed, wq):
    rows = normed.shape[0]
    return pl.pallas_call(
        query_kernel,
        out_shape=jax.ShapeDtypeStruct((wq.shape[1] // HD, rows, HD), BF),
        in_specs=[vmem_spec()] * 2,
        out_specs=vmem_spec(),
        compiler_params=params(8),
        name="queries",
    )(normed, wq)


def attend_kernel(first, last, places, depth, sizes, *refs):
    refs = list(refs)
    valid_counts, own = refs.pop(0), refs.pop(0)
    query = refs.pop(0)
    chunks = [refs.pop(0) for _ in sizes]
    if not first:
        top_in, sums_in = refs.pop(0), refs.pop(0)
    if last:
        w_out = refs.pop(0)
        mixed = refs.pop(0)
        top_out, sums_out = refs.pop(0), refs.pop(0)
    else:
        top_out, sums_out = refs.pop(0), refs.pop(0)
    heads, rows, _ = query.shape
    here = own[0]
    here_y, here_z, here_core = lax.div(here, 2 * depth), lax.rem(lax.div(here, 2), depth), lax.rem(here, 2)
    behind = 2 * here_core - 1
    pages = []
    for chunk, size in zip(chunks, sizes):
        for index in range(size):
            side, shift, core = places[len(pages)]
            place = lax.rem(here_z + depth + shift * behind, depth)
            number = (here_y ^ side) * (2 * depth) + place * 2 + (here_core ^ core)
            pages.append((chunk, index, valid_counts[number]))
    group_size = 4 if len(pages) in (4, 7, 8) else min(3, len(pages))
    tokens = chunks[0].shape[1]
    lane = lax.broadcasted_iota(jnp.int32, (1, tokens), 1)
    lane_kv = lax.broadcasted_iota(jnp.int32, (tokens, 2 * HD), 1)
    fresh = first
    for begin in range(0, len(pages), group_size):
        group = pages[begin : begin + group_size]
        keys, values, masks = [], [], []
        for chunk, index, count in group:
            both = chunk[index]
            keys.append(both[:, HD : 2 * HD])
            values.append(jnp.where(lane_kv < HD, both, jnp.ones_like(both)))
            masks.append(jnp.where(lane < count, 0.0, NEG).astype(F32))
        for head in range(heads):
            scores = [
                lax.dot_general(query[head], key, (((1,), (1,)), ((), ())), preferred_element_type=F32) + mask
                for key, mask in zip(keys, masks)
            ]
            largest = functools.reduce(jnp.maximum, scores)
            top = jnp.max(largest, axis=1, keepdims=True)
            if not fresh:
                source_top, source_sums = (top_in, sums_in) if begin == 0 else (top_out, sums_out)
                before = source_top[head][:, 0:1]
                top = jnp.maximum(top, before)
                carried = source_sums[head] * jnp.exp2(before - top)
            total = functools.reduce(
                jnp.add,
                [
                    jnp.dot(jnp.exp2(score - top).astype(BF), value, preferred_element_type=F32)
                    for score, value in zip(scores, values)
                ],
            )
            if not fresh:
                total = total + carried
            sums_out[head] = total
            top_out[head] = jnp.broadcast_to(top, (rows, HD))
        fresh = False
    if last:
        attended = jnp.concatenate(
            [(sums_out[head][:, 0:HD] / sums_out[head][:, HD : 2 * HD]).astype(BF) for head in range(heads)], axis=1
        )
        mixed[...] = jnp.dot(attended, w_out[...], preferred_element_type=F32).astype(BF)


def attend(valid_counts, own, depth, query, pieces, carry=None, w_out=None):
    heads, rows, _ = query.shape
    chunks = [piece[0] for piece in pieces]
    places = [place for piece in pieces for place in piece[1]]
    sizes = tuple(chunk.shape[0] for chunk in chunks)
    state = [jax.ShapeDtypeStruct((heads, rows, HD), F32), jax.ShapeDtypeStruct((heads, rows, 2 * HD), F32)]
    operands = [valid_counts, own, query, *chunks]
    if carry is not None:
        operands += list(carry)
    scratch = []
    if w_out is not None:
        operands.append(w_out)
        out_shape = [jax.ShapeDtypeStruct((rows, w_out.shape[1]), BF)]
        scratch = [pltpu.VMEM(one.shape, F32) for one in state]
    else:
        out_shape = state
    pairs = sum(sizes) * chunks[0].shape[1] * heads * rows
    return pl.pallas_call(
        functools.partial(attend_kernel, carry is None, w_out is not None, places, depth, sizes),
        out_shape=out_shape,
        in_specs=[smem_spec()] * 2 + [vmem_spec()] * (len(operands) - 2),
        out_specs=[vmem_spec()] * len(out_shape),
        scratch_shapes=scratch,
        cost_estimate=pl.CostEstimate(flops=pairs // 8, transcendentals=0, bytes_accessed=2**16),
        compiler_params=params(14),
        name="attend",
    )(*operands)


def total_kernel(parts, out):
    total = parts[0].astype(F32)
    for part in range(1, parts.shape[0]):
        total = total + parts[part].astype(F32)
    out[...] = total.astype(BF)


def total_of(parts):
    return pl.pallas_call(
        total_kernel,
        out_shape=jax.ShapeDtypeStruct(parts.shape[1:], BF),
        in_specs=[vmem_spec()],
        out_specs=vmem_spec(),
        compiler_params=params(8),
        name="total",
    )(parts)


def per_device(
    pages,
    valid_counts,
    dw_weight,
    dw_bias,
    norm1_gain,
    fc1_w,
    fc1_b,
    fc2_w,
    fc2_b,
    layer_scale,
    norm2_gain,
    w_query,
    w_key,
    w_value,
    w_out,
):
    channels = pages.shape[-1]
    rows = pages.shape[1] * pages.shape[2]
    groups = lax.axis_size("head")
    blocks = lax.axis_size("blk")
    depth = blocks // 4
    share = rows // groups

    def moved(array, target):
        return lax.ppermute(array, "blk", [(i, target(i)) for i in range(blocks)])

    def flip_y(array):
        return moved(array, lambda i: (i + 2 * depth) % blocks)

    def flip_core(array):
        return moved(array, lambda i: i ^ 1)

    def along_z(array, step=1):
        def target(i):
            turn = 2 * step if i % 2 == 0 else -2 * step
            return i // (2 * depth) * (2 * depth) + (i + turn) % (2 * depth)

        return moved(array, target)

    own = lax.axis_index("blk").astype(jnp.int32)[None]
    place = lax.axis_index("head").astype(jnp.int32)[None]
    hold = lax.optimization_barrier

    partial = mlp(pages, dw_weight, dw_bias, norm1_gain, fc1_w, fc1_b, fc2_w)
    parts = lax.all_to_all(partial.reshape(groups, share, channels), "head", 0, 0, tiled=True)
    copies = block_norm(place, parts, pages.reshape(rows, channels), layer_scale, fc2_b, norm2_gain)
    normed = lax.all_to_all(copies, "head", 0, 0, tiled=True).reshape(rows, channels)

    def fold(pieces, carry=None, weight=None):
        return attend(valid_counts, own, depth, query, pieces, carry, weight)

    def mine(side, shift):
        return [(side, shift, 0), (side, shift, 1)]

    def theirs(side, shift):
        return [(side, -shift, 1), (side, -shift, 0)]

    start = key_values(normed, w_key, w_value)
    beside = flip_core(start)
    query = queries_of(normed, w_query)
    beside, query = hold((beside, query))
    own_pair = jnp.concatenate([start, beside])

    first = along_z(own_pair)
    own_other = flip_y(own_pair)
    carry = fold([(own_pair, mine(0, 0))])
    first, own_other, carry = hold((first, own_other, carry))

    second = along_z(first)
    first_other = flip_y(first)
    first_core = flip_core(first)
    carry = fold([(own_other, mine(1, 0)), (first, mine(0, 1))], carry)
    second, first_other, first_core, carry = hold((second, first_other, first_core, carry))

    third = along_z(second)
    second_other = flip_y(second)
    second_core = flip_core(second)
    first_other_core = flip_core(first_other)
    carry = fold([(first_core, theirs(0, 1)), (first_other, mine(1, 1)), (second, mine(0, 2))], carry)
    third, second_other, second_core, first_other_core, carry = hold(
        (third, second_other, second_core, first_other_core, carry)
    )

    third_other = flip_y(third)
    far = along_z(third[0:1])
    far_other = along_z(second_other[0:1], 2)
    third_core = flip_core(third)
    second_other_core = flip_core(second_other)
    carry = fold(
        [
            (first_other_core, theirs(1, 1)),
            (second_core, theirs(0, 2)),
            (second_other, mine(1, 2)),
            (third, mine(0, 3)),
        ],
        carry,
    )
    third_core, second_other_core, carry = hold((third_core, second_other_core, carry))
    carry = fold([(third_core, theirs(0, 3)), (second_other_core, theirs(1, 2))], carry)
    third_other, far, far_other, carry = hold((third_other, far, far_other, carry))

    last = jnp.concatenate([third_other, far, far_other])
    last_core = flip_core(last)
    carry = fold([(last, mine(1, 3) + [(0, depth // 2, 0), (1, depth // 2, 0)])], carry)
    last_core, carry = hold((last_core, carry))
    (mixed,) = fold([(last_core, theirs(1, 3) + [(0, depth // 2, 1), (1, depth // 2, 1)])], carry, w_out)
    parts = lax.all_to_all(mixed.reshape(groups, share, channels), "head", 0, 0, tiled=True)
    return total_of(parts)


def solution(mesh):
    in_specs = (
        P("blk", None, None, None),
        P(),
        P(),
        P(),
        P(),
        P(None, "head"),
        P("head"),
        P("head", None),
        P(),
        P(),
        P(),
        P(None, "head"),
        P(None, "head"),
        P(None, "head"),
        P("head", None),
    )
    out_specs = P(("blk", "head"), None)
    return jax.shard_map(per_device, mesh=mesh, in_specs=in_specs, out_specs=out_specs, check_vma=False)
```

```python
import functools

import jax
import jax.numpy as jnp
from jax import lax
from jax.experimental import pallas as pl
from jax.experimental.pallas import tpu as pltpu
from jax.sharding import PartitionSpec as P

HEADS = 32
KV_HEADS = 8
HD = 128
LANES = 128
LOG2E = 1.4426950408889634
NEG = -1e30
BF = jnp.bfloat16
F32 = jnp.float32


def params(mebibytes):
    return pltpu.CompilerParams(vmem_limit_bytes=mebibytes * 2**20)


def vmem_spec():
    return pl.BlockSpec(memory_space=pltpu.VMEM)


def smem_spec():
    return pl.BlockSpec(memory_space=pltpu.SMEM)


def fold_lanes(pieces):
    return jnp.sum(functools.reduce(jnp.add, pieces), axis=-1, keepdims=True)


def normalise(pieces, gain, epsilon):
    width = len(pieces) * pieces[0].shape[-1]
    mean = fold_lanes(pieces) / width
    centred = [piece - mean for piece in pieces]
    spread = fold_lanes([piece * piece for piece in centred]) / width
    factor = lax.rsqrt(spread + epsilon)
    return [(piece * factor * gain[index : index + 1, :]).astype(BF) for index, piece in enumerate(centred)]


def fixed(array):
    return pltpu.with_memory_space_constraint(array, pltpu.HBM)


def lane_rows(vector):
    return vector.reshape(-1, LANES)


def mlp_kernel(pages_hbm, dw_hbm, dwb_hbm, gain_hbm, w1_hbm, b1_hbm, w2_hbm, out, *scratch):
    padded, conv, pages, dw, dwb, gain, w1, b1, w2, arrived = scratch
    pairs = (
        (w1_hbm, w1),
        (w2_hbm, w2),
        (b1_hbm, b1),
        (gain_hbm, gain),
        (dwb_hbm, dwb),
        (dw_hbm, dw),
        (pages_hbm, pages),
    )
    loads = [pltpu.make_async_copy(source, target, arrived.at[index]) for index, (source, target) in enumerate(pairs)]
    for load in reversed(loads):
        load.start()
    for load in loads[2:]:
        load.wait()
    height, breadth, channels = pages.shape
    half = height // 2
    column = lax.broadcasted_iota(jnp.int32, (half, breadth, LANES), 1)
    blank = jnp.zeros((3, breadth, LANES), F32)
    for chunk in range(channels // LANES):
        lanes = slice(chunk * LANES, (chunk + 1) * LANES)
        padded[chunk, 0:3] = blank
        padded[chunk, 3 + height : 6 + height] = blank
        padded[chunk, 3 : 3 + height] = pages[:, :, lanes].astype(F32)
        for top in range(0, height, half):
            total = jnp.broadcast_to(dwb[chunk : chunk + 1, :][None], (half, breadth, LANES))
            for sideways in range(7):
                product = None
                for vertical in range(7):
                    tap = dw[vertical, sideways : sideways + 1, lanes][None]
                    term = padded[chunk, top + vertical : top + vertical + half] * tap
                    product = term if product is None else product + term
                offset = sideways - 3
                if offset:
                    rolled = pltpu.roll(product, (-offset) % breadth, axis=1)
                    inside = (column + offset >= 0) if offset < 0 else (column + offset < breadth)
                    product = jnp.where(inside, rolled, 0.0)
                total = total + product
            conv[chunk, top * breadth : (top + half) * breadth] = total.reshape(half * breadth, LANES)
    normed = normalise([conv[chunk] for chunk in range(channels // LANES)], gain, 1e-06)
    loads[0].wait()
    product = jnp.dot(jnp.concatenate(normed, axis=1), w1[...], preferred_element_type=F32)
    hidden = []
    for chunk in range(product.shape[1] // LANES):
        pre = product[:, chunk * LANES : (chunk + 1) * LANES] + b1[chunk : chunk + 1, :]
        hidden.append((0.5 * pre * (1.0 + lax.erf(pre * 0.7071067811865476))).astype(BF))
    loads[1].wait()
    out[...] = jnp.dot(jnp.concatenate(hidden, axis=1), w2[...], preferred_element_type=F32).astype(BF)


def mlp(pages, dw, dwb, gain, w1, b1, w2):
    _, height, breadth, channels = pages.shape
    rows = height * breadth
    operands = (pages[0], dw, lane_rows(dwb), lane_rows(gain), w1, lane_rows(b1), w2)
    return pl.pallas_call(
        mlp_kernel,
        out_shape=jax.ShapeDtypeStruct((rows, channels), BF),
        in_specs=[pl.BlockSpec(memory_space=pltpu.HBM)] * 7,
        out_specs=vmem_spec(),
        scratch_shapes=[
            pltpu.VMEM((channels // LANES, height + 6, breadth, LANES), F32),
            pltpu.VMEM((channels // LANES, rows, LANES), F32),
            *[pltpu.VMEM(operand.shape, operand.dtype) for operand in operands],
            pltpu.SemaphoreType.DMA((7,)),
        ],
        compiler_params=params(16),
        name="conv_mlp",
    )(*[fixed(operand) for operand in operands])


def block_kernel(place, parts, pages, packed, out):
    count, chunk, channels = parts.shape
    pieces = channels // LANES
    scale, b2 = packed[0:pieces, :], packed[pieces : 2 * pieces, :]
    start = pl.multiple_of(place[0] * chunk, chunk)
    block = []
    for index in range(channels // LANES):
        lanes = slice(index * LANES, (index + 1) * LANES)
        row = slice(index, index + 1)
        total = functools.reduce(jnp.add, [parts[part, :, lanes].astype(F32) for part in range(count)])
        own = pages[pl.ds(start, chunk), lanes].astype(F32)
        block.append(own + scale[row, :] * (total + b2[row, :]))
    normed = jnp.concatenate(normalise(block, packed.at[2 * pieces : 3 * pieces, :], 1e-05), axis=1)
    for part in range(count):
        out[part] = normed


def block_norm(place, parts, pages, scale, b2, gain):
    return pl.pallas_call(
        block_kernel,
        out_shape=jax.ShapeDtypeStruct(parts.shape, BF),
        in_specs=[smem_spec()] + [vmem_spec()] * 3,
        out_specs=vmem_spec(),
        compiler_params=params(8),
        name="block_norm",
    )(place, parts, pages, jnp.concatenate([lane_rows(scale), lane_rows(b2), lane_rows(gain)]))


def kv_kernel(normed, wk, wv, out):
    tokens = normed[...]
    out[0, :, 0:HD] = jnp.dot(tokens, wv[...], preferred_element_type=F32).astype(BF)
    out[0, :, HD : 2 * HD] = jnp.dot(tokens, wk[...], preferred_element_type=F32).astype(BF)


def key_values(normed, wk, wv):
    rows = normed.shape[0]
    return pl.pallas_call(
        kv_kernel,
        out_shape=jax.ShapeDtypeStruct((1, rows, 2 * HD), BF),
        in_specs=[vmem_spec()] * 3,
        out_specs=vmem_spec(),
        compiler_params=params(8),
        name="key_values",
    )(normed, wk, wv)


def query_kernel(_, normed, wq, out):
    product = jnp.dot(normed[...], wq[...], preferred_element_type=F32) * (HD**-0.5 * LOG2E)
    for head in range(out.shape[0]):
        out[head] = product[:, head * HD : (head + 1) * HD].astype(BF)


def queries_of(valid_counts, normed, wq):
    rows = normed.shape[0]
    return pl.pallas_call(
        query_kernel,
        out_shape=jax.ShapeDtypeStruct((wq.shape[1] // HD, rows, HD), BF),
        in_specs=[smem_spec()] + [vmem_spec()] * 2,
        out_specs=vmem_spec(),
        compiler_params=params(8),
        name="queries",
    )(valid_counts, normed, wq)


def attend_kernel(first, last, places, depth, sizes, *refs):
    refs = list(refs)
    valid_counts, own = refs.pop(0), refs.pop(0)
    query = refs.pop(0)
    chunks = [refs.pop(0) for _ in sizes]
    if not first:
        top_in, sums_in = refs.pop(0), refs.pop(0)
    if last:
        w_out = refs.pop(0)
        mixed = refs.pop(0)
        top_out, sums_out = refs.pop(0), refs.pop(0)
    else:
        top_out, sums_out = refs.pop(0), refs.pop(0)
    heads, rows, _ = query.shape
    here = own[0]
    here_y, here_z, here_core = lax.div(here, 2 * depth), lax.rem(lax.div(here, 2), depth), lax.rem(here, 2)
    behind = 2 * here_core - 1
    pages = []
    for chunk, size in zip(chunks, sizes):
        for index in range(size):
            side, shift, core = places[len(pages)]
            place = lax.rem(here_z + depth + shift * behind, depth)
            number = (here_y ^ side) * (2 * depth) + place * 2 + (here_core ^ core)
            pages.append((chunk, index, valid_counts[number]))
    group_size = 4 if len(pages) in (4, 7, 8) else min(3, len(pages))
    tokens = chunks[0].shape[1]
    lane = lax.broadcasted_iota(jnp.int32, (1, tokens), 1)
    lane_kv = lax.broadcasted_iota(jnp.int32, (tokens, 2 * HD), 1)
    fresh = first
    for begin in range(0, len(pages), group_size):
        group = pages[begin : begin + group_size]
        keys, values, masks = [], [], []
        for chunk, index, count in group:
            both = chunk[index]
            keys.append(both[:, HD : 2 * HD])
            values.append(jnp.where(lane_kv < HD, both, jnp.ones_like(both)))
            masks.append(jnp.where(lane < count, 0.0, NEG).astype(F32))
        for head in range(heads):
            scores = [
                lax.dot_general(query[head], key, (((1,), (1,)), ((), ())), preferred_element_type=F32) + mask
                for key, mask in zip(keys, masks)
            ]
            largest = functools.reduce(jnp.maximum, scores)
            top = jnp.broadcast_to(jnp.max(largest, axis=1, keepdims=True), (rows, HD))
            if not fresh:
                source_top, source_sums = (top_in, sums_in) if begin == 0 else (top_out, sums_out)
                before = source_top[head]
                top = jnp.maximum(top, before)
                factor = jnp.exp2(before - top)
                carried = source_sums[head] * jnp.concatenate([factor, factor], axis=1)
            wide_top = jnp.concatenate([top] * (tokens // HD), axis=1)
            total = functools.reduce(
                jnp.add,
                [
                    jnp.dot(jnp.exp2(score - wide_top).astype(BF), value, preferred_element_type=F32)
                    for score, value in zip(scores, values)
                ],
            )
            if not fresh:
                total = total + carried
            sums_out[head] = total
            top_out[head] = top
        fresh = False
    if last:
        attended = jnp.concatenate(
            [(sums_out[head][:, 0:HD] / sums_out[head][:, HD : 2 * HD]).astype(BF) for head in range(heads)], axis=1
        )
        mixed[...] = jnp.dot(attended, w_out[...], preferred_element_type=F32).astype(BF)


def attend(valid_counts, own, depth, query, pieces, carry=None, w_out=None):
    heads, rows, _ = query.shape
    chunks = [piece[0] for piece in pieces]
    places = [place for piece in pieces for place in piece[1]]
    sizes = tuple(chunk.shape[0] for chunk in chunks)
    state = [jax.ShapeDtypeStruct((heads, rows, HD), F32), jax.ShapeDtypeStruct((heads, rows, 2 * HD), F32)]
    operands = [valid_counts, own, query, *chunks]
    if carry is not None:
        operands += list(carry)
    scratch = []
    if w_out is not None:
        operands.append(w_out)
        out_shape = [jax.ShapeDtypeStruct((rows, w_out.shape[1]), BF)]
        scratch = [pltpu.VMEM(one.shape, F32) for one in state]
    else:
        out_shape = state
    pairs = sum(sizes) * chunks[0].shape[1] * heads * rows
    return pl.pallas_call(
        functools.partial(attend_kernel, carry is None, w_out is not None, places, depth, sizes),
        out_shape=out_shape,
        in_specs=[smem_spec()] * 2 + [vmem_spec()] * (len(operands) - 2),
        out_specs=[vmem_spec()] * len(out_shape),
        scratch_shapes=scratch,
        cost_estimate=pl.CostEstimate(flops=pairs // 8, transcendentals=0, bytes_accessed=2**16),
        compiler_params=params(14),
        name="attend",
    )(*operands)


def total_kernel(parts, out):
    total = parts[0].astype(F32)
    for part in range(1, parts.shape[0]):
        total = total + parts[part].astype(F32)
    out[...] = total.astype(BF)


def total_of(parts):
    return pl.pallas_call(
        total_kernel,
        out_shape=jax.ShapeDtypeStruct(parts.shape[1:], BF),
        in_specs=[vmem_spec()],
        out_specs=vmem_spec(),
        compiler_params=params(8),
        name="total",
    )(parts)


def per_device(
    pages,
    valid_counts,
    dw_weight,
    dw_bias,
    norm1_gain,
    fc1_w,
    fc1_b,
    fc2_w,
    fc2_b,
    layer_scale,
    norm2_gain,
    w_query,
    w_key,
    w_value,
    w_out,
):
    channels = pages.shape[-1]
    rows = pages.shape[1] * pages.shape[2]
    groups = lax.axis_size("head")
    blocks = lax.axis_size("blk")
    depth = blocks // 4
    share = rows // groups

    def moved(array, target):
        return lax.ppermute(array, "blk", [(i, target(i)) for i in range(blocks)])

    def flip_y(array):
        return moved(array, lambda i: (i + 2 * depth) % blocks)

    def flip_core(array):
        return moved(array, lambda i: i ^ 1)

    def along_z(array, step=1):
        def target(i):
            turn = 2 * step if i % 2 == 0 else -2 * step
            return i // (2 * depth) * (2 * depth) + (i + turn) % (2 * depth)

        return moved(array, target)

    own = lax.axis_index("blk").astype(jnp.int32)[None]
    place = lax.axis_index("head").astype(jnp.int32)[None]
    hold = lax.optimization_barrier

    partial = mlp(pages, dw_weight, dw_bias, norm1_gain, fc1_w, fc1_b, fc2_w)
    parts = lax.all_to_all(partial.reshape(groups, share, channels), "head", 0, 0, tiled=True)
    copies = block_norm(place, parts, pages.reshape(rows, channels), layer_scale, fc2_b, norm2_gain)
    normed = lax.all_to_all(copies, "head", 0, 0, tiled=True).reshape(rows, channels)

    def fold(pieces, carry=None, weight=None):
        return attend(valid_counts, own, depth, query, pieces, carry, weight)

    def mine(side, shift):
        return [(side, shift, 0), (side, shift, 1)]

    def theirs(side, shift):
        return [(side, -shift, 1), (side, -shift, 0)]

    start = key_values(normed, w_key, w_value)
    beside = flip_core(start)
    other = flip_y(start)
    query = queries_of(valid_counts, normed, w_query)
    beside, query = hold((beside, query))
    own_pair = jnp.concatenate([start, beside])

    first = along_z(own_pair)
    carry = fold([(own_pair, mine(0, 0))])
    first, other, carry = hold((first, other, carry))

    second = along_z(jnp.concatenate([first, other]))
    first_other = flip_y(first[1:2])
    other_core = flip_core(other)
    first_core = flip_core(first)
    carry = fold([(other, [(1, 0, 0)]), (first, mine(0, 1))], carry)
    second, first_other, other_core, first_core, carry = hold((second, first_other, other_core, first_core, carry))

    third = along_z(second)
    second_other = flip_y(second[1:2])
    second_core = flip_core(second)
    first_other_core = flip_core(first_other)
    carry = fold(
        [
            (other_core, [(1, 0, 1)]),
            (first_core, theirs(0, 1)),
            (first_other, [(1, 1, 1)]),
            (second, mine(0, 2) + [(1, 1, 0)]),
        ],
        carry,
    )
    third, second_other, second_core, first_other_core, carry = hold(
        (third, second_other, second_core, first_other_core, carry)
    )

    fourth = along_z(third[1:3])
    third_other = flip_y(third[1:2])
    far_other = along_z(third[2:3], 2)
    third_core = flip_core(third)
    second_other_core = flip_core(second_other)
    carry = fold(
        [
            (second_core, theirs(0, 2) + [(1, -1, 1)]),
            (first_other_core, [(1, -1, 0)]),
            (second_other, [(1, 2, 1)]),
            (third, mine(0, 3) + [(1, 2, 0)]),
        ],
        carry,
    )
    third_core, second_other_core, carry = hold((third_core, second_other_core, carry))
    carry = fold([(third_core, theirs(0, 3) + [(1, -2, 1)]), (second_other_core, [(1, -2, 0)])], carry)
    fourth, third_other, far_other, carry = hold((fourth, third_other, far_other, carry))

    half = depth // 2
    last = jnp.concatenate([fourth, third_other, far_other])
    last_core = flip_core(last)
    carry = fold([(last, [(0, half, 1), (1, 3, 0), (1, 3, 1), (1, half, 0)])], carry)
    last_core, carry = hold((last_core, carry))
    (mixed,) = fold([(last_core, [(0, -half, 0), (1, -3, 1), (1, -3, 0), (1, -half, 1)])], carry, w_out)
    parts = lax.all_to_all(mixed.reshape(groups, share, channels), "head", 0, 0, tiled=True)
    return total_of(parts)


def solution(mesh):
    in_specs = (
        P("blk", None, None, None),
        P(),
        P(),
        P(),
        P(),
        P(None, "head"),
        P("head"),
        P("head", None),
        P(),
        P(),
        P(),
        P(None, "head"),
        P(None, "head"),
        P(None, "head"),
        P("head", None),
    )
    out_specs = P(("blk", "head"), None)
    return jax.shard_map(per_device, mesh=mesh, in_specs=in_specs, out_specs=out_specs, check_vma=False)
```

```python
import functools

import jax
import jax.numpy as jnp
from jax import lax
from jax.experimental import pallas as pl
from jax.experimental.pallas import tpu as pltpu
from jax.sharding import PartitionSpec as P

HEADS = 32
KV_HEADS = 8
HD = 128
LANES = 128
LOG2E = 1.4426950408889634
NEG = -1e30
BF = jnp.bfloat16
F32 = jnp.float32


def params(mebibytes):
    return pltpu.CompilerParams(vmem_limit_bytes=mebibytes * 2**20)


def vmem_spec():
    return pl.BlockSpec(memory_space=pltpu.VMEM)


def smem_spec():
    return pl.BlockSpec(memory_space=pltpu.SMEM)


def fold_lanes(pieces):
    return jnp.sum(functools.reduce(jnp.add, pieces), axis=-1, keepdims=True)


def normalise(pieces, gain, epsilon):
    width = len(pieces) * pieces[0].shape[-1]
    mean = fold_lanes(pieces) / width
    centred = [piece - mean for piece in pieces]
    spread = fold_lanes([piece * piece for piece in centred]) / width
    factor = lax.rsqrt(spread + epsilon)
    return [(piece * factor * gain[index : index + 1, :]).astype(BF) for index, piece in enumerate(centred)]


def fixed(array):
    return pltpu.with_memory_space_constraint(array, pltpu.HBM)


def lane_rows(vector):
    return vector.reshape(-1, LANES)


def mlp_kernel(pages_hbm, dw_hbm, dwb_hbm, gain_hbm, w1_hbm, b1_hbm, w2_hbm, out, *scratch):
    padded, conv, pages, dw, dwb, gain, w1, b1, w2, arrived = scratch
    pairs = (
        (w1_hbm, w1),
        (w2_hbm, w2),
        (b1_hbm, b1),
        (gain_hbm, gain),
        (dwb_hbm, dwb),
        (dw_hbm, dw),
        (pages_hbm, pages),
    )
    loads = [pltpu.make_async_copy(source, target, arrived.at[index]) for index, (source, target) in enumerate(pairs)]
    for load in reversed(loads):
        load.start()
    for load in loads[2:]:
        load.wait()
    height, breadth, channels = pages.shape
    half = height // 2
    column = lax.broadcasted_iota(jnp.int32, (half, breadth, LANES), 1)
    blank = jnp.zeros((3, breadth, LANES), F32)
    for chunk in range(channels // LANES):
        lanes = slice(chunk * LANES, (chunk + 1) * LANES)
        padded[chunk, 0:3] = blank
        padded[chunk, 3 + height : 6 + height] = blank
        padded[chunk, 3 : 3 + height] = pages[:, :, lanes].astype(F32)
        for top in range(0, height, half):
            total = jnp.broadcast_to(dwb[chunk : chunk + 1, :][None], (half, breadth, LANES))
            for sideways in range(7):
                product = None
                for vertical in range(7):
                    tap = dw[vertical, sideways : sideways + 1, lanes][None]
                    term = padded[chunk, top + vertical : top + vertical + half] * tap
                    product = term if product is None else product + term
                offset = sideways - 3
                if offset:
                    rolled = pltpu.roll(product, (-offset) % breadth, axis=1)
                    inside = (column + offset >= 0) if offset < 0 else (column + offset < breadth)
                    product = jnp.where(inside, rolled, 0.0)
                total = total + product
            conv[chunk, top * breadth : (top + half) * breadth] = total.reshape(half * breadth, LANES)
    normed = normalise([conv[chunk] for chunk in range(channels // LANES)], gain, 1e-06)
    loads[0].wait()
    product = jnp.dot(jnp.concatenate(normed, axis=1), w1[...], preferred_element_type=F32)
    hidden = []
    for chunk in range(product.shape[1] // LANES):
        pre = product[:, chunk * LANES : (chunk + 1) * LANES] + b1[chunk : chunk + 1, :]
        hidden.append((0.5 * pre * (1.0 + lax.erf(pre * 0.7071067811865476))).astype(BF))
    loads[1].wait()
    out[...] = jnp.dot(jnp.concatenate(hidden, axis=1), w2[...], preferred_element_type=F32).astype(BF)


def mlp(pages, dw, dwb, gain, w1, b1, w2):
    _, height, breadth, channels = pages.shape
    rows = height * breadth
    operands = (pages[0], dw, lane_rows(dwb), lane_rows(gain), w1, lane_rows(b1), w2)
    return pl.pallas_call(
        mlp_kernel,
        out_shape=jax.ShapeDtypeStruct((rows, channels), BF),
        in_specs=[pl.BlockSpec(memory_space=pltpu.HBM)] * 7,
        out_specs=vmem_spec(),
        scratch_shapes=[
            pltpu.VMEM((channels // LANES, height + 6, breadth, LANES), F32),
            pltpu.VMEM((channels // LANES, rows, LANES), F32),
            *[pltpu.VMEM(operand.shape, operand.dtype) for operand in operands],
            pltpu.SemaphoreType.DMA((7,)),
        ],
        compiler_params=params(16),
        name="conv_mlp",
    )(*[fixed(operand) for operand in operands])


def block_kernel(place, parts, pages, packed, out):
    count, chunk, channels = parts.shape
    pieces = channels // LANES
    scale, b2 = packed[0:pieces, :], packed[pieces : 2 * pieces, :]
    start = pl.multiple_of(place[0] * chunk, chunk)
    block = []
    for index in range(channels // LANES):
        lanes = slice(index * LANES, (index + 1) * LANES)
        row = slice(index, index + 1)
        total = functools.reduce(jnp.add, [parts[part, :, lanes].astype(F32) for part in range(count)])
        own = pages[pl.ds(start, chunk), lanes].astype(F32)
        block.append(own + scale[row, :] * (total + b2[row, :]))
    normed = jnp.concatenate(normalise(block, packed.at[2 * pieces : 3 * pieces, :], 1e-05), axis=1)
    for part in range(count):
        out[part] = normed


def block_norm(place, parts, pages, scale, b2, gain):
    return pl.pallas_call(
        block_kernel,
        out_shape=jax.ShapeDtypeStruct(parts.shape, BF),
        in_specs=[smem_spec()] + [vmem_spec()] * 3,
        out_specs=vmem_spec(),
        compiler_params=params(8),
        name="block_norm",
    )(place, parts, pages, jnp.concatenate([lane_rows(scale), lane_rows(b2), lane_rows(gain)]))


def kv_kernel(normed, wk, wv, out):
    tokens = normed[...]
    out[0, :, 0:HD] = jnp.dot(tokens, wv[...], preferred_element_type=F32).astype(BF)
    out[0, :, HD : 2 * HD] = jnp.dot(tokens, wk[...], preferred_element_type=F32).astype(BF)


def key_values(normed, wk, wv):
    rows = normed.shape[0]
    return pl.pallas_call(
        kv_kernel,
        out_shape=jax.ShapeDtypeStruct((1, rows, 2 * HD), BF),
        in_specs=[vmem_spec()] * 3,
        out_specs=vmem_spec(),
        compiler_params=params(8),
        name="key_values",
    )(normed, wk, wv)


def query_kernel(_, normed, wq, out):
    product = jnp.dot(normed[...], wq[...], preferred_element_type=F32) * (HD**-0.5 * LOG2E)
    for head in range(out.shape[0]):
        out[head] = product[:, head * HD : (head + 1) * HD].astype(BF)


def queries_of(valid_counts, normed, wq):
    rows = normed.shape[0]
    return pl.pallas_call(
        query_kernel,
        out_shape=jax.ShapeDtypeStruct((wq.shape[1] // HD, rows, HD), BF),
        in_specs=[smem_spec()] + [vmem_spec()] * 2,
        out_specs=vmem_spec(),
        compiler_params=params(8),
        name="queries",
    )(valid_counts, normed, wq)


def attend_kernel(first, last, places, depth, sizes, *refs):
    refs = list(refs)
    valid_counts, own = refs.pop(0), refs.pop(0)
    query = refs.pop(0)
    chunks = [refs.pop(0) for _ in sizes]
    if not first:
        top_in, sums_in = refs.pop(0), refs.pop(0)
    if last:
        w_out = refs.pop(0)
        mixed = refs.pop(0)
        top_out, sums_out = refs.pop(0), refs.pop(0)
    else:
        top_out, sums_out = refs.pop(0), refs.pop(0)
    heads, rows, _ = query.shape
    here = own[0]
    here_y, here_z, here_core = lax.div(here, 2 * depth), lax.rem(lax.div(here, 2), depth), lax.rem(here, 2)
    behind = 2 * here_core - 1
    pages = []
    for chunk, size in zip(chunks, sizes):
        for index in range(size):
            side, shift, core = places[len(pages)]
            place = lax.rem(here_z + depth + shift * behind, depth)
            number = (here_y ^ side) * (2 * depth) + place * 2 + (here_core ^ core)
            pages.append((chunk, index, valid_counts[number]))
    group_size = 4 if len(pages) in (4, 7, 8) else min(3, len(pages))
    tokens = chunks[0].shape[1]
    lane = lax.broadcasted_iota(jnp.int32, (1, tokens), 1)
    lane_kv = lax.broadcasted_iota(jnp.int32, (tokens, 2 * HD), 1)
    fresh = first
    for begin in range(0, len(pages), group_size):
        group = pages[begin : begin + group_size]
        keys, values, masks = [], [], []
        for chunk, index, count in group:
            both = chunk[index]
            keys.append(both[:, HD : 2 * HD])
            values.append(jnp.where(lane_kv < HD, both, jnp.ones_like(both)))
            masks.append(jnp.where(lane < count, 0.0, NEG).astype(F32))
        for head in range(heads):
            scores = [
                lax.dot_general(query[head], key, (((1,), (1,)), ((), ())), preferred_element_type=F32) + mask
                for key, mask in zip(keys, masks)
            ]
            largest = functools.reduce(jnp.maximum, scores)
            top = jnp.broadcast_to(jnp.max(largest, axis=1, keepdims=True), (rows, HD))
            if not fresh:
                source_top, source_sums = (top_in, sums_in) if begin == 0 else (top_out, sums_out)
                before = source_top[head]
                top = jnp.maximum(top, before)
                factor = jnp.exp2(before - top)
                carried = source_sums[head] * jnp.concatenate([factor, factor], axis=1)
            wide_top = jnp.concatenate([top] * (tokens // HD), axis=1)
            total = functools.reduce(
                jnp.add,
                [
                    jnp.dot(jnp.exp2(score - wide_top).astype(BF), value, preferred_element_type=F32)
                    for score, value in zip(scores, values)
                ],
            )
            if not fresh:
                total = total + carried
            sums_out[head] = total
            top_out[head] = top
        fresh = False
    if last:
        attended = jnp.concatenate(
            [(sums_out[head][:, 0:HD] / sums_out[head][:, HD : 2 * HD]).astype(BF) for head in range(heads)], axis=1
        )
        mixed[...] = jnp.dot(attended, w_out[...], preferred_element_type=F32).astype(BF)


def attend(valid_counts, own, depth, query, pieces, carry=None, w_out=None):
    heads, rows, _ = query.shape
    chunks = [piece[0] for piece in pieces]
    places = [place for piece in pieces for place in piece[1]]
    sizes = tuple(chunk.shape[0] for chunk in chunks)
    state = [jax.ShapeDtypeStruct((heads, rows, HD), F32), jax.ShapeDtypeStruct((heads, rows, 2 * HD), F32)]
    operands = [valid_counts, own, query, *chunks]
    if carry is not None:
        operands += list(carry)
    scratch = []
    if w_out is not None:
        operands.append(w_out)
        out_shape = [jax.ShapeDtypeStruct((rows, w_out.shape[1]), BF)]
        scratch = [pltpu.VMEM(one.shape, F32) for one in state]
    else:
        out_shape = state
    pairs = sum(sizes) * chunks[0].shape[1] * heads * rows
    return pl.pallas_call(
        functools.partial(attend_kernel, carry is None, w_out is not None, places, depth, sizes),
        out_shape=out_shape,
        in_specs=[smem_spec()] * 2 + [vmem_spec()] * (len(operands) - 2),
        out_specs=[vmem_spec()] * len(out_shape),
        scratch_shapes=scratch,
        cost_estimate=pl.CostEstimate(flops=pairs // 8, transcendentals=0, bytes_accessed=2**16),
        compiler_params=params(14),
        name="attend",
    )(*operands)


def total_kernel(parts, out):
    total = parts[0].astype(F32)
    for part in range(1, parts.shape[0]):
        total = total + parts[part].astype(F32)
    out[...] = total.astype(BF)


def total_of(parts):
    return pl.pallas_call(
        total_kernel,
        out_shape=jax.ShapeDtypeStruct(parts.shape[1:], BF),
        in_specs=[vmem_spec()],
        out_specs=vmem_spec(),
        compiler_params=params(8),
        name="total",
    )(parts)


def per_device(
    pages,
    valid_counts,
    dw_weight,
    dw_bias,
    norm1_gain,
    fc1_w,
    fc1_b,
    fc2_w,
    fc2_b,
    layer_scale,
    norm2_gain,
    w_query,
    w_key,
    w_value,
    w_out,
):
    channels = pages.shape[-1]
    rows = pages.shape[1] * pages.shape[2]
    groups = lax.axis_size("head")
    blocks = lax.axis_size("blk")
    depth = blocks // 4
    share = rows // groups

    def moved(array, target):
        return lax.ppermute(array, "blk", [(i, target(i)) for i in range(blocks)])

    def flip_y(array):
        return moved(array, lambda i: (i + 2 * depth) % blocks)

    def flip_core(array):
        return moved(array, lambda i: i ^ 1)

    def along_z(array, step=1):
        def target(i):
            turn = 2 * step if i % 2 == 0 else -2 * step
            return i // (2 * depth) * (2 * depth) + (i + turn) % (2 * depth)

        return moved(array, target)

    own = lax.axis_index("blk").astype(jnp.int32)[None]
    place = lax.axis_index("head").astype(jnp.int32)[None]
    hold = lax.optimization_barrier

    partial = mlp(pages, dw_weight, dw_bias, norm1_gain, fc1_w, fc1_b, fc2_w)
    parts = lax.all_to_all(partial.reshape(groups, share, channels), "head", 0, 0, tiled=True)
    copies = block_norm(place, parts, pages.reshape(rows, channels), layer_scale, fc2_b, norm2_gain)
    normed = lax.all_to_all(copies, "head", 0, 0, tiled=True).reshape(rows, channels)

    def fold(pieces, carry=None, weight=None):
        return attend(valid_counts, own, depth, query, pieces, carry, weight)

    def crossed(places):
        return [(side, -shift, 1 - core) for side, shift, core in places]

    def both_cores(pieces, carry, weight=None):
        arrays = [piece[0] for piece in pieces]
        places = [place for piece in pieces for place in piece[1]]
        joined = arrays[0] if len(arrays) == 1 else jnp.concatenate(arrays)
        exchanged = flip_core(joined)
        carry = fold([(joined, places)], carry)
        exchanged, carry = hold((exchanged, carry))
        return fold([(exchanged, crossed(places))], carry, weight)

    start = key_values(normed, w_key, w_value)
    beside = flip_core(start)
    other = flip_y(start)
    query = queries_of(valid_counts, normed, w_query)
    beside, query = hold((beside, query))
    own_pair = jnp.concatenate([start, beside])

    one = along_z(own_pair)
    carry = fold([(own_pair, [(0, 0, 0), (0, 0, 1)])])
    one, other, carry = hold((one, other, carry))

    one_other = flip_y(one[1:2])
    joined = jnp.concatenate([one, other])
    two = along_z(joined)
    carry = both_cores([(joined, [(0, 1, 0), (0, 1, 1), (1, 0, 0)])], carry)
    two, one_other, carry = hold((two, one_other, carry))

    three = along_z(two)
    two_other = flip_y(two[1:2])
    carry = both_cores([(two, [(0, 2, 0), (0, 2, 1), (1, 1, 0)]), (one_other, [(1, 1, 1)])], carry)
    three, two_other, carry = hold((three, two_other, carry))

    half = depth // 2
    four = along_z(three[1:3])
    three_other = flip_y(three[1:2])
    far_other = along_z(three[2:3], 2)
    carry = both_cores([(three, [(0, 3, 0), (0, 3, 1), (1, 2, 0)]), (two_other, [(1, 2, 1)])], carry)
    four, three_other, far_other, carry = hold((four, three_other, far_other, carry))

    pieces = [(four, [(0, half, 1), (1, 3, 0)]), (three_other, [(1, 3, 1)]), (far_other, [(1, half, 0)])]
    (mixed,) = both_cores(pieces, carry, w_out)
    parts = lax.all_to_all(mixed.reshape(groups, share, channels), "head", 0, 0, tiled=True)
    return total_of(parts)


def solution(mesh):
    in_specs = (
        P("blk", None, None, None),
        P(),
        P(),
        P(),
        P(),
        P(None, "head"),
        P("head"),
        P("head", None),
        P(),
        P(),
        P(),
        P(None, "head"),
        P(None, "head"),
        P(None, "head"),
        P("head", None),
    )
    out_specs = P(("blk", "head"), None)
    return jax.shard_map(per_device, mesh=mesh, in_specs=in_specs, out_specs=out_specs, check_vma=False)
```

```python
import functools

import jax
import jax.numpy as jnp
from jax import lax
from jax.experimental import pallas as pl
from jax.experimental.pallas import tpu as pltpu
from jax.sharding import PartitionSpec as P

HEADS = 32
KV_HEADS = 8
HD = 128
LANES = 128
LOG2E = 1.4426950408889634
NEG = -1e30
BF = jnp.bfloat16
F32 = jnp.float32


def params(mebibytes):
    return pltpu.CompilerParams(vmem_limit_bytes=mebibytes * 2**20)


def vmem_spec():
    return pl.BlockSpec(memory_space=pltpu.VMEM)


def smem_spec():
    return pl.BlockSpec(memory_space=pltpu.SMEM)


def fold_lanes(pieces):
    return jnp.sum(functools.reduce(jnp.add, pieces), axis=-1, keepdims=True)


def normalise(pieces, gain, epsilon):
    width = len(pieces) * pieces[0].shape[-1]
    mean = fold_lanes(pieces) / width
    centred = [piece - mean for piece in pieces]
    spread = fold_lanes([piece * piece for piece in centred]) / width
    factor = lax.rsqrt(spread + epsilon)
    return [(piece * factor * gain[index : index + 1, :]).astype(BF) for index, piece in enumerate(centred)]


def fixed(array):
    return pltpu.with_memory_space_constraint(array, pltpu.HBM)


def lane_rows(vector):
    return vector.reshape(-1, LANES)


def mlp_kernel(pages_hbm, dw_hbm, dwb_hbm, gain_hbm, w1_hbm, b1_hbm, w2_hbm, out, *scratch):
    padded, conv, pages, dw, dwb, gain, w1, b1, w2, arrived = scratch
    pairs = (
        (w1_hbm, w1),
        (w2_hbm, w2),
        (b1_hbm, b1),
        (gain_hbm, gain),
        (dwb_hbm, dwb),
        (dw_hbm, dw),
        (pages_hbm, pages),
    )
    loads = [pltpu.make_async_copy(source, target, arrived.at[index]) for index, (source, target) in enumerate(pairs)]
    for load in reversed(loads):
        load.start()
    for load in loads[2:]:
        load.wait()
    height, breadth, channels = pages.shape
    half = height // 2
    column = lax.broadcasted_iota(jnp.int32, (half, breadth, LANES), 1)
    blank = jnp.zeros((3, breadth, LANES), F32)
    for chunk in range(channels // LANES):
        lanes = slice(chunk * LANES, (chunk + 1) * LANES)
        padded[chunk, 0:3] = blank
        padded[chunk, 3 + height : 6 + height] = blank
        padded[chunk, 3 : 3 + height] = pages[:, :, lanes].astype(F32)
        for top in range(0, height, half):
            total = jnp.broadcast_to(dwb[chunk : chunk + 1, :][None], (half, breadth, LANES))
            for sideways in range(7):
                product = None
                for vertical in range(7):
                    tap = dw[vertical, sideways : sideways + 1, lanes][None]
                    term = padded[chunk, top + vertical : top + vertical + half] * tap
                    product = term if product is None else product + term
                offset = sideways - 3
                if offset:
                    rolled = pltpu.roll(product, (-offset) % breadth, axis=1)
                    inside = (column + offset >= 0) if offset < 0 else (column + offset < breadth)
                    product = jnp.where(inside, rolled, 0.0)
                total = total + product
            conv[chunk, top * breadth : (top + half) * breadth] = total.reshape(half * breadth, LANES)
    normed = normalise([conv[chunk] for chunk in range(channels // LANES)], gain, 1e-06)
    loads[0].wait()
    product = jnp.dot(jnp.concatenate(normed, axis=1), w1[...], preferred_element_type=F32)
    hidden = []
    for chunk in range(product.shape[1] // LANES):
        pre = product[:, chunk * LANES : (chunk + 1) * LANES] + b1[chunk : chunk + 1, :]
        hidden.append((0.5 * pre * (1.0 + lax.erf(pre * 0.7071067811865476))).astype(BF))
    loads[1].wait()
    out[...] = jnp.dot(jnp.concatenate(hidden, axis=1), w2[...], preferred_element_type=F32).astype(BF)


def mlp(pages, dw, dwb, gain, w1, b1, w2):
    _, height, breadth, channels = pages.shape
    rows = height * breadth
    operands = (pages[0], dw, lane_rows(dwb), lane_rows(gain), w1, lane_rows(b1), w2)
    return pl.pallas_call(
        mlp_kernel,
        out_shape=jax.ShapeDtypeStruct((rows, channels), BF),
        in_specs=[pl.BlockSpec(memory_space=pltpu.HBM)] * 7,
        out_specs=vmem_spec(),
        scratch_shapes=[
            pltpu.VMEM((channels // LANES, height + 6, breadth, LANES), F32),
            pltpu.VMEM((channels // LANES, rows, LANES), F32),
            *[pltpu.VMEM(operand.shape, operand.dtype) for operand in operands],
            pltpu.SemaphoreType.DMA((7,)),
        ],
        compiler_params=params(16),
        name="conv_mlp",
    )(*[fixed(operand) for operand in operands])


def block_kernel(place, parts, pages, packed, out):
    count, chunk, channels = parts.shape
    pieces = channels // LANES
    scale, b2 = packed[0:pieces, :], packed[pieces : 2 * pieces, :]
    start = pl.multiple_of(place[0] * chunk, chunk)
    block = []
    for index in range(channels // LANES):
        lanes = slice(index * LANES, (index + 1) * LANES)
        row = slice(index, index + 1)
        total = functools.reduce(jnp.add, [parts[part, :, lanes].astype(F32) for part in range(count)])
        own = pages[pl.ds(start, chunk), lanes].astype(F32)
        block.append(own + scale[row, :] * (total + b2[row, :]))
    normed = jnp.concatenate(normalise(block, packed.at[2 * pieces : 3 * pieces, :], 1e-05), axis=1)
    for part in range(count):
        out[part] = normed


def block_norm(place, parts, pages, scale, b2, gain):
    return pl.pallas_call(
        block_kernel,
        out_shape=jax.ShapeDtypeStruct(parts.shape, BF),
        in_specs=[smem_spec()] + [vmem_spec()] * 3,
        out_specs=vmem_spec(),
        compiler_params=params(8),
        name="block_norm",
    )(place, parts, pages, jnp.concatenate([lane_rows(scale), lane_rows(b2), lane_rows(gain)]))


def kv_kernel(normed, wk, wv, out):
    tokens = normed[...]
    out[0, :, 0:HD] = jnp.dot(tokens, wv[...], preferred_element_type=F32).astype(BF)
    out[0, :, HD : 2 * HD] = jnp.dot(tokens, wk[...], preferred_element_type=F32).astype(BF)


def key_values(normed, wk, wv):
    rows = normed.shape[0]
    return pl.pallas_call(
        kv_kernel,
        out_shape=jax.ShapeDtypeStruct((1, rows, 2 * HD), BF),
        in_specs=[vmem_spec()] * 3,
        out_specs=vmem_spec(),
        compiler_params=params(8),
        name="key_values",
    )(normed, wk, wv)


def query_kernel(_, normed, wq, out):
    product = jnp.dot(normed[...], wq[...], preferred_element_type=F32) * (HD**-0.5 * LOG2E)
    for head in range(out.shape[0]):
        out[head] = product[:, head * HD : (head + 1) * HD].astype(BF)


def queries_of(valid_counts, normed, wq):
    rows = normed.shape[0]
    return pl.pallas_call(
        query_kernel,
        out_shape=jax.ShapeDtypeStruct((wq.shape[1] // HD, rows, HD), BF),
        in_specs=[smem_spec()] + [vmem_spec()] * 2,
        out_specs=vmem_spec(),
        compiler_params=params(8),
        name="queries",
    )(valid_counts, normed, wq)


def attend_kernel(first, last, places, depth, sizes, *refs):
    refs = list(refs)
    valid_counts, own = refs.pop(0), refs.pop(0)
    query = refs.pop(0)
    chunks = [refs.pop(0) for _ in sizes]
    if not first:
        top_in, sums_in = refs.pop(0), refs.pop(0)
    if last:
        w_out = refs.pop(0)
        mixed = refs.pop(0)
        top_out, sums_out = refs.pop(0), refs.pop(0)
    else:
        top_out, sums_out = refs.pop(0), refs.pop(0)
    heads, rows, _ = query.shape
    here = own[0]
    here_y, here_z, here_core = lax.div(here, 2 * depth), lax.rem(lax.div(here, 2), depth), lax.rem(here, 2)
    behind = 2 * here_core - 1
    pages = []
    for chunk, size in zip(chunks, sizes):
        for index in range(size):
            side, shift, core = places[len(pages)]
            place = lax.rem(here_z + depth + shift * behind, depth)
            number = (here_y ^ side) * (2 * depth) + place * 2 + (here_core ^ core)
            pages.append((chunk, index, valid_counts[number]))
    group_size = 4 if len(pages) in (4, 7, 8) else min(3, len(pages))
    tokens = chunks[0].shape[1]
    lane = lax.broadcasted_iota(jnp.int32, (1, tokens), 1)
    lane_kv = lax.broadcasted_iota(jnp.int32, (tokens, 2 * HD), 1)
    fresh = first
    for begin in range(0, len(pages), group_size):
        group = pages[begin : begin + group_size]
        keys, values, masks = [], [], []
        for chunk, index, count in group:
            both = chunk[index]
            keys.append(both[:, HD : 2 * HD])
            values.append(jnp.where(lane_kv < HD, both, jnp.ones_like(both)))
            masks.append(jnp.where(lane < count, 0.0, NEG).astype(F32))
        for head in range(heads):
            scores = [
                lax.dot_general(query[head], key, (((1,), (1,)), ((), ())), preferred_element_type=F32) + mask
                for key, mask in zip(keys, masks)
            ]
            largest = functools.reduce(jnp.maximum, scores)
            top = jnp.broadcast_to(jnp.max(largest, axis=1, keepdims=True), (rows, HD))
            if not fresh:
                source_top, source_sums = (top_in, sums_in) if begin == 0 else (top_out, sums_out)
                before = source_top[head]
                top = jnp.maximum(top, before)
                factor = jnp.exp2(before - top)
                carried = source_sums[head] * jnp.concatenate([factor, factor], axis=1)
            wide_top = jnp.concatenate([top] * (tokens // HD), axis=1)
            total = functools.reduce(
                jnp.add,
                [
                    jnp.dot(jnp.exp2(score - wide_top).astype(BF), value, preferred_element_type=F32)
                    for score, value in zip(scores, values)
                ],
            )
            if not fresh:
                total = total + carried
            sums_out[head] = total
            top_out[head] = top
        fresh = False
    if last:
        attended = jnp.concatenate(
            [(sums_out[head][:, 0:HD] / sums_out[head][:, HD : 2 * HD]).astype(BF) for head in range(heads)], axis=1
        )
        mixed[...] = jnp.dot(attended, w_out[...], preferred_element_type=F32).astype(BF)


def attend(valid_counts, own, depth, query, pieces, carry=None, w_out=None):
    heads, rows, _ = query.shape
    chunks = [piece[0] for piece in pieces]
    places = [place for piece in pieces for place in piece[1]]
    sizes = tuple(chunk.shape[0] for chunk in chunks)
    state = [jax.ShapeDtypeStruct((heads, rows, HD), F32), jax.ShapeDtypeStruct((heads, rows, 2 * HD), F32)]
    operands = [valid_counts, own, query, *chunks]
    if carry is not None:
        operands += list(carry)
    scratch = []
    if w_out is not None:
        operands.append(w_out)
        out_shape = [jax.ShapeDtypeStruct((rows, w_out.shape[1]), BF)]
        scratch = [pltpu.VMEM(one.shape, F32) for one in state]
    else:
        out_shape = state
    pairs = sum(sizes) * chunks[0].shape[1] * heads * rows
    return pl.pallas_call(
        functools.partial(attend_kernel, carry is None, w_out is not None, places, depth, sizes),
        out_shape=out_shape,
        in_specs=[smem_spec()] * 2 + [vmem_spec()] * (len(operands) - 2),
        out_specs=[vmem_spec()] * len(out_shape),
        scratch_shapes=scratch,
        cost_estimate=pl.CostEstimate(flops=pairs // 8, transcendentals=0, bytes_accessed=2**16),
        compiler_params=params(14),
        name="attend",
    )(*operands)


def total_kernel(parts, out):
    total = parts[0].astype(F32)
    for part in range(1, parts.shape[0]):
        total = total + parts[part].astype(F32)
    out[...] = total.astype(BF)


def total_of(parts):
    return pl.pallas_call(
        total_kernel,
        out_shape=jax.ShapeDtypeStruct(parts.shape[1:], BF),
        in_specs=[vmem_spec()],
        out_specs=vmem_spec(),
        compiler_params=params(8),
        name="total",
    )(parts)


def per_device(
    pages,
    valid_counts,
    dw_weight,
    dw_bias,
    norm1_gain,
    fc1_w,
    fc1_b,
    fc2_w,
    fc2_b,
    layer_scale,
    norm2_gain,
    w_query,
    w_key,
    w_value,
    w_out,
):
    channels = pages.shape[-1]
    rows = pages.shape[1] * pages.shape[2]
    groups = lax.axis_size("head")
    blocks = lax.axis_size("blk")
    depth = blocks // 4
    share = rows // groups

    def moved(array, target):
        return lax.ppermute(array, "blk", [(i, target(i)) for i in range(blocks)])

    def flip_y(array):
        return moved(array, lambda i: (i + 2 * depth) % blocks)

    def flip_core(array):
        return moved(array, lambda i: i ^ 1)

    def along_z(array, step=1):
        def target(i):
            turn = 2 * step if i % 2 == 0 else -2 * step
            return i // (2 * depth) * (2 * depth) + (i + turn) % (2 * depth)

        return moved(array, target)

    own = lax.axis_index("blk").astype(jnp.int32)[None]
    place = lax.axis_index("head").astype(jnp.int32)[None]
    hold = lax.optimization_barrier

    partial = mlp(pages, dw_weight, dw_bias, norm1_gain, fc1_w, fc1_b, fc2_w)
    parts = lax.all_to_all(partial.reshape(groups, share, channels), "head", 0, 0, tiled=True)
    copies = block_norm(place, parts, pages.reshape(rows, channels), layer_scale, fc2_b, norm2_gain)
    normed = lax.all_to_all(copies, "head", 0, 0, tiled=True).reshape(rows, channels)

    def fold(pieces, carry=None, weight=None):
        return attend(valid_counts, own, depth, query, pieces, carry, weight)

    def crossed(places):
        return [(side, -shift, 1 - core) for side, shift, core in places]

    def both_cores(pieces, shared, carry, weight=None):
        exchanged = [flip_core(array) for array, _ in shared]
        carry = fold(pieces, carry)
        exchanged, carry = hold((exchanged, carry))
        return fold([(array, crossed(piece[1])) for array, piece in zip(exchanged, shared)], carry, weight)

    def halves(trio, places, single, place):
        joined = jnp.concatenate([trio[2:3], single])
        return [(trio[0:2], places[0:2]), (joined, [places[2], place])]

    start = key_values(normed, w_key, w_value)
    beside = flip_core(start)
    other = flip_y(start)
    query = queries_of(valid_counts, normed, w_query)
    beside, query = hold((beside, query))
    own_pair = jnp.concatenate([start, beside])

    one = along_z(own_pair)
    carry = fold([(own_pair, [(0, 0, 0), (0, 0, 1)])])
    one, other, carry = hold((one, other, carry))

    two = along_z(jnp.concatenate([one, other]))
    one_other = flip_y(one[1:2])
    pieces = [(one, [(0, 1, 0), (0, 1, 1)]), (other, [(1, 0, 0)])]
    carry = both_cores(pieces, pieces, carry)
    two, one_other, carry = hold((two, one_other, carry))

    three = along_z(two)
    two_other = flip_y(two[1:2])
    places, place = [(0, 2, 0), (0, 2, 1), (1, 1, 0)], (1, 1, 1)
    carry = both_cores([(two, places), (one_other, [place])], halves(two, places, one_other, place), carry)
    three, two_other, carry = hold((three, two_other, carry))

    four = along_z(three)
    three_other = flip_y(three[1:2])
    far_other = along_z(three[2:3], 2)
    places, place = [(0, 3, 0), (0, 3, 1), (1, 2, 0)], (1, 2, 1)
    carry = both_cores([(three, places), (two_other, [place])], halves(three, places, two_other, place), carry)
    four, three_other, far_other, carry = hold((four, three_other, far_other, carry))

    half = depth // 2
    places = [(1, 3, 0), (1, 3, 1), (1, half, 0)]
    pieces = [
        (four, [(0, half, 0), (0, half, 1), places[0]]),
        (three_other, [places[1]]),
        (far_other, [places[2]]),
    ]
    shared = jnp.concatenate([four[2:3], three_other, far_other])
    (mixed,) = both_cores(pieces, [(shared, places)], carry, w_out)
    parts = lax.all_to_all(mixed.reshape(groups, share, channels), "head", 0, 0, tiled=True)
    return total_of(parts)


def solution(mesh):
    in_specs = (
        P("blk", None, None, None),
        P(),
        P(),
        P(),
        P(),
        P(None, "head"),
        P("head"),
        P("head", None),
        P(),
        P(),
        P(),
        P(None, "head"),
        P(None, "head"),
        P(None, "head"),
        P("head", None),
    )
    out_specs = P(("blk", "head"), None)
    return jax.shard_map(per_device, mesh=mesh, in_specs=in_specs, out_specs=out_specs, check_vma=False)
```

```python
import functools

import jax
import jax.numpy as jnp
from jax import lax
from jax.experimental import pallas as pl
from jax.experimental.pallas import tpu as pltpu
from jax.sharding import PartitionSpec as P

HEADS = 32
KV_HEADS = 8
HD = 128
LANES = 128
LOG2E = 1.4426950408889634
NEG = -1e30
BF = jnp.bfloat16
F32 = jnp.float32


def params(mebibytes):
    return pltpu.CompilerParams(vmem_limit_bytes=mebibytes * 2**20)


def vmem_spec():
    return pl.BlockSpec(memory_space=pltpu.VMEM)


def smem_spec():
    return pl.BlockSpec(memory_space=pltpu.SMEM)


def fold_lanes(pieces):
    return jnp.sum(functools.reduce(jnp.add, pieces), axis=-1, keepdims=True)


def normalise(pieces, gain, epsilon):
    width = len(pieces) * pieces[0].shape[-1]
    mean = fold_lanes(pieces) / width
    centred = [piece - mean for piece in pieces]
    spread = fold_lanes([piece * piece for piece in centred]) / width
    factor = lax.rsqrt(spread + epsilon)
    return [(piece * factor * gain[index : index + 1, :]).astype(BF) for index, piece in enumerate(centred)]


def fixed(array):
    return pltpu.with_memory_space_constraint(array, pltpu.HBM)


def lane_rows(vector):
    return vector.reshape(-1, LANES)


def mlp_kernel(pages_hbm, dw_hbm, dwb_hbm, gain_hbm, w1_hbm, b1_hbm, w2_hbm, out, *scratch):
    padded, conv, pages, dw, dwb, gain, w1, b1, w2, arrived = scratch
    pairs = (
        (w1_hbm, w1),
        (w2_hbm, w2),
        (b1_hbm, b1),
        (gain_hbm, gain),
        (dwb_hbm, dwb),
        (dw_hbm, dw),
        (pages_hbm, pages),
    )
    loads = [pltpu.make_async_copy(source, target, arrived.at[index]) for index, (source, target) in enumerate(pairs)]
    for load in reversed(loads):
        load.start()
    for load in loads[2:]:
        load.wait()
    height, breadth, channels = pages.shape
    half = height // 2
    column = lax.broadcasted_iota(jnp.int32, (half, breadth, LANES), 1)
    blank = jnp.zeros((3, breadth, LANES), F32)
    for chunk in range(channels // LANES):
        lanes = slice(chunk * LANES, (chunk + 1) * LANES)
        padded[chunk, 0:3] = blank
        padded[chunk, 3 + height : 6 + height] = blank
        padded[chunk, 3 : 3 + height] = pages[:, :, lanes].astype(F32)
        for top in range(0, height, half):
            total = jnp.broadcast_to(dwb[chunk : chunk + 1, :][None], (half, breadth, LANES))
            for sideways in range(7):
                product = None
                for vertical in range(7):
                    tap = dw[vertical, sideways : sideways + 1, lanes][None]
                    term = padded[chunk, top + vertical : top + vertical + half] * tap
                    product = term if product is None else product + term
                offset = sideways - 3
                if offset:
                    rolled = pltpu.roll(product, (-offset) % breadth, axis=1)
                    inside = (column + offset >= 0) if offset < 0 else (column + offset < breadth)
                    product = jnp.where(inside, rolled, 0.0)
                total = total + product
            conv[chunk, top * breadth : (top + half) * breadth] = total.reshape(half * breadth, LANES)
    normed = normalise([conv[chunk] for chunk in range(channels // LANES)], gain, 1e-06)
    loads[0].wait()
    product = jnp.dot(jnp.concatenate(normed, axis=1), w1[...], preferred_element_type=F32)
    hidden = []
    for chunk in range(product.shape[1] // LANES):
        pre = product[:, chunk * LANES : (chunk + 1) * LANES] + b1[chunk : chunk + 1, :]
        hidden.append((0.5 * pre * (1.0 + lax.erf(pre * 0.7071067811865476))).astype(BF))
    loads[1].wait()
    out[...] = jnp.dot(jnp.concatenate(hidden, axis=1), w2[...], preferred_element_type=F32).astype(BF)


def mlp(pages, dw, dwb, gain, w1, b1, w2):
    _, height, breadth, channels = pages.shape
    rows = height * breadth
    operands = (pages[0], dw, lane_rows(dwb), lane_rows(gain), w1, lane_rows(b1), w2)
    return pl.pallas_call(
        mlp_kernel,
        out_shape=jax.ShapeDtypeStruct((rows, channels), BF),
        in_specs=[pl.BlockSpec(memory_space=pltpu.HBM)] * 7,
        out_specs=vmem_spec(),
        scratch_shapes=[
            pltpu.VMEM((channels // LANES, height + 6, breadth, LANES), F32),
            pltpu.VMEM((channels // LANES, rows, LANES), F32),
            *[pltpu.VMEM(operand.shape, operand.dtype) for operand in operands],
            pltpu.SemaphoreType.DMA((7,)),
        ],
        compiler_params=params(16),
        name="conv_mlp",
    )(*[fixed(operand) for operand in operands])


def block_kernel(place, parts, pages, packed, out):
    count, chunk, channels = parts.shape
    pieces = channels // LANES
    scale, b2 = packed[0:pieces, :], packed[pieces : 2 * pieces, :]
    start = pl.multiple_of(place[0] * chunk, chunk)
    block = []
    for index in range(channels // LANES):
        lanes = slice(index * LANES, (index + 1) * LANES)
        row = slice(index, index + 1)
        total = functools.reduce(jnp.add, [parts[part, :, lanes].astype(F32) for part in range(count)])
        own = pages[pl.ds(start, chunk), lanes].astype(F32)
        block.append(own + scale[row, :] * (total + b2[row, :]))
    normed = jnp.concatenate(normalise(block, packed.at[2 * pieces : 3 * pieces, :], 1e-05), axis=1)
    for part in range(count):
        out[part] = normed


def block_norm(place, parts, pages, scale, b2, gain):
    return pl.pallas_call(
        block_kernel,
        out_shape=jax.ShapeDtypeStruct(parts.shape, BF),
        in_specs=[smem_spec()] + [vmem_spec()] * 3,
        out_specs=vmem_spec(),
        compiler_params=params(8),
        name="block_norm",
    )(place, parts, pages, jnp.concatenate([lane_rows(scale), lane_rows(b2), lane_rows(gain)]))


def kv_kernel(normed, wk, wv, out):
    tokens = normed[...]
    out[0, :, 0:HD] = jnp.dot(tokens, wv[...], preferred_element_type=F32).astype(BF)
    out[0, :, HD : 2 * HD] = jnp.dot(tokens, wk[...], preferred_element_type=F32).astype(BF)


def key_values(normed, wk, wv):
    rows = normed.shape[0]
    return pl.pallas_call(
        kv_kernel,
        out_shape=jax.ShapeDtypeStruct((1, rows, 2 * HD), BF),
        in_specs=[vmem_spec()] * 3,
        out_specs=vmem_spec(),
        compiler_params=params(8),
        name="key_values",
    )(normed, wk, wv)


def query_kernel(_, normed, wq, out):
    product = jnp.dot(normed[...], wq[...], preferred_element_type=F32) * (HD**-0.5 * LOG2E)
    for head in range(out.shape[0]):
        out[head] = product[:, head * HD : (head + 1) * HD].astype(BF)


def queries_of(valid_counts, normed, wq):
    rows = normed.shape[0]
    return pl.pallas_call(
        query_kernel,
        out_shape=jax.ShapeDtypeStruct((wq.shape[1] // HD, rows, HD), BF),
        in_specs=[smem_spec()] + [vmem_spec()] * 2,
        out_specs=vmem_spec(),
        compiler_params=params(8),
        name="queries",
    )(valid_counts, normed, wq)


def attend_kernel(first, last, places, depth, sizes, *refs):
    refs = list(refs)
    valid_counts, own = refs.pop(0), refs.pop(0)
    query = refs.pop(0)
    chunks = [refs.pop(0) for _ in sizes]
    if not first:
        top_in, sums_in = refs.pop(0), refs.pop(0)
    if last:
        w_out = refs.pop(0)
        mixed = refs.pop(0)
        top_out, sums_out = refs.pop(0), refs.pop(0)
    else:
        top_out, sums_out = refs.pop(0), refs.pop(0)
    heads, rows, _ = query.shape
    here = own[0]
    here_y, here_z, here_core = lax.div(here, 2 * depth), lax.rem(lax.div(here, 2), depth), lax.rem(here, 2)
    behind = 2 * here_core - 1
    pages = []
    for chunk, size in zip(chunks, sizes):
        for index in range(size):
            side, shift, core = places[len(pages)]
            place = lax.rem(here_z + depth + shift * behind, depth)
            number = (here_y ^ side) * (2 * depth) + place * 2 + (here_core ^ core)
            pages.append((chunk, index, valid_counts[number]))
    group_size = 4 if len(pages) in (4, 7, 8) else min(3, len(pages))
    tokens = chunks[0].shape[1]
    lane = lax.broadcasted_iota(jnp.int32, (1, tokens), 1)
    lane_kv = lax.broadcasted_iota(jnp.int32, (tokens, 2 * HD), 1)
    fresh = first
    for begin in range(0, len(pages), group_size):
        group = pages[begin : begin + group_size]
        keys, values, masks = [], [], []
        for chunk, index, count in group:
            both = chunk[index]
            keys.append(both[:, HD : 2 * HD])
            values.append(jnp.where(lane_kv < HD, both, jnp.ones_like(both)))
            masks.append(jnp.where(lane < count, 0.0, NEG).astype(F32))
        for head in range(heads):
            scores = [
                lax.dot_general(query[head], key, (((1,), (1,)), ((), ())), preferred_element_type=F32) + mask
                for key, mask in zip(keys, masks)
            ]
            largest = functools.reduce(jnp.maximum, scores)
            top = jnp.broadcast_to(jnp.max(largest, axis=1, keepdims=True), (rows, HD))
            if not fresh:
                source_top, source_sums = (top_in, sums_in) if begin == 0 else (top_out, sums_out)
                before = source_top[head]
                top = jnp.maximum(top, before)
                factor = jnp.exp2(before - top)
                carried = source_sums[head] * jnp.concatenate([factor, factor], axis=1)
            wide_top = jnp.concatenate([top] * (tokens // HD), axis=1)
            total = functools.reduce(
                jnp.add,
                [
                    jnp.dot(jnp.exp2(score - wide_top).astype(BF), value, preferred_element_type=F32)
                    for score, value in zip(scores, values)
                ],
            )
            if not fresh:
                total = total + carried
            sums_out[head] = total
            top_out[head] = top
        fresh = False
    if last:
        attended = jnp.concatenate(
            [(sums_out[head][:, 0:HD] / sums_out[head][:, HD : 2 * HD]).astype(BF) for head in range(heads)], axis=1
        )
        mixed[...] = jnp.dot(attended, w_out[...], preferred_element_type=F32).astype(BF)


def attend(valid_counts, own, depth, query, pieces, carry=None, w_out=None):
    heads, rows, _ = query.shape
    chunks = [piece[0] for piece in pieces]
    places = [place for piece in pieces for place in piece[1]]
    sizes = tuple(chunk.shape[0] for chunk in chunks)
    state = [jax.ShapeDtypeStruct((heads, rows, HD), F32), jax.ShapeDtypeStruct((heads, rows, 2 * HD), F32)]
    operands = [valid_counts, own, query, *chunks]
    if carry is not None:
        operands += list(carry)
    scratch = []
    if w_out is not None:
        operands.append(w_out)
        out_shape = [jax.ShapeDtypeStruct((rows, w_out.shape[1]), BF)]
        scratch = [pltpu.VMEM(one.shape, F32) for one in state]
    else:
        out_shape = state
    pairs = sum(sizes) * chunks[0].shape[1] * heads * rows
    return pl.pallas_call(
        functools.partial(attend_kernel, carry is None, w_out is not None, places, depth, sizes),
        out_shape=out_shape,
        in_specs=[smem_spec()] * 2 + [vmem_spec()] * (len(operands) - 2),
        out_specs=[vmem_spec()] * len(out_shape),
        scratch_shapes=scratch,
        cost_estimate=pl.CostEstimate(flops=pairs // 8, transcendentals=0, bytes_accessed=2**16),
        compiler_params=params(14),
        name="attend",
    )(*operands)


def total_kernel(parts, out):
    total = parts[0].astype(F32)
    for part in range(1, parts.shape[0]):
        total = total + parts[part].astype(F32)
    out[...] = total.astype(BF)


def total_of(parts):
    return pl.pallas_call(
        total_kernel,
        out_shape=jax.ShapeDtypeStruct(parts.shape[1:], BF),
        in_specs=[vmem_spec()],
        out_specs=vmem_spec(),
        compiler_params=params(8),
        name="total",
    )(parts)


def per_device(
    pages,
    valid_counts,
    dw_weight,
    dw_bias,
    norm1_gain,
    fc1_w,
    fc1_b,
    fc2_w,
    fc2_b,
    layer_scale,
    norm2_gain,
    w_query,
    w_key,
    w_value,
    w_out,
):
    channels = pages.shape[-1]
    rows = pages.shape[1] * pages.shape[2]
    groups = lax.axis_size("head")
    blocks = lax.axis_size("blk")
    depth = blocks // 4
    share = rows // groups

    def moved(array, target):
        return lax.ppermute(array, "blk", [(i, target(i)) for i in range(blocks)])

    def flip_y(array):
        return moved(array, lambda i: (i + 2 * depth) % blocks)

    def flip_core(array):
        return moved(array, lambda i: i ^ 1)

    def along_z(array, step=1):
        def target(i):
            turn = 2 * step if i % 2 == 0 else -2 * step
            return i // (2 * depth) * (2 * depth) + (i + turn) % (2 * depth)

        return moved(array, target)

    own = lax.axis_index("blk").astype(jnp.int32)[None]
    place = lax.axis_index("head").astype(jnp.int32)[None]
    hold = lax.optimization_barrier

    partial = mlp(pages, dw_weight, dw_bias, norm1_gain, fc1_w, fc1_b, fc2_w)
    parts = lax.all_to_all(partial.reshape(groups, share, channels), "head", 0, 0, tiled=True)
    copies = block_norm(place, parts, pages.reshape(rows, channels), layer_scale, fc2_b, norm2_gain)
    normed = lax.all_to_all(copies, "head", 0, 0, tiled=True).reshape(rows, channels)

    def fold(pieces, carry=None, weight=None):
        return attend(valid_counts, own, depth, query, pieces, carry, weight)

    def crossed(places):
        return [(side, -shift, 1 - core) for side, shift, core in places]

    def both_cores(pieces, shared, carry, weight=None):
        exchanged = [flip_core(array) for array, _ in shared]
        carry = fold(pieces, carry)
        exchanged, carry = hold((exchanged, carry))
        return fold([(array, crossed(piece[1])) for array, piece in zip(exchanged, shared)], carry, weight)

    def halves(trio, places, single, place):
        joined = jnp.concatenate([trio[2:3], single])
        return [(trio[0:2], places[0:2]), (joined, [places[2], place])]

    start = key_values(normed, w_key, w_value)
    beside = flip_core(start)
    other = flip_y(start)
    query = queries_of(valid_counts, normed, w_query)
    beside, query = hold((beside, query))
    own_pair = jnp.concatenate([start, beside])

    one = along_z(own_pair)
    carry = fold([(own_pair, [(0, 0, 0), (0, 0, 1)])])
    one, other, carry = hold((one, other, carry))

    two = along_z(jnp.concatenate([one, other]))
    one_other = flip_y(one[1:2])
    pieces = [(one, [(0, 1, 0), (0, 1, 1)]), (other, [(1, 0, 0)])]
    carry = both_cores(pieces, pieces, carry)
    two, one_other, carry = hold((two, one_other, carry))

    three = along_z(two)
    two_other = flip_y(two[1:2])
    places, place = [(0, 2, 0), (0, 2, 1), (1, 1, 0)], (1, 1, 1)
    carry = both_cores([(two, places), (one_other, [place])], halves(two, places, one_other, place), carry)
    three, two_other, carry = hold((three, two_other, carry))

    half = depth // 2
    four = along_z(three[1:3])
    three_other = flip_y(three[1:2])
    far_other = along_z(three[2:3], 2)
    joined = jnp.concatenate([three, two_other])
    pieces = [(joined, [(0, 3, 0), (0, 3, 1), (1, 2, 0), (1, 2, 1)])]
    carry = both_cores(pieces, pieces, carry)
    four, three_other, far_other, carry = hold((four, three_other, far_other, carry))

    joined = jnp.concatenate([four, three_other, far_other])
    pieces = [(joined, [(0, half, 1), (1, 3, 0), (1, 3, 1), (1, half, 0)])]
    (mixed,) = both_cores(pieces, pieces, carry, w_out)
    parts = lax.all_to_all(mixed.reshape(groups, share, channels), "head", 0, 0, tiled=True)
    return total_of(parts)


def solution(mesh):
    in_specs = (
        P("blk", None, None, None),
        P(),
        P(),
        P(),
        P(),
        P(None, "head"),
        P("head"),
        P("head", None),
        P(),
        P(),
        P(),
        P(None, "head"),
        P(None, "head"),
        P(None, "head"),
        P("head", None),
    )
    out_specs = P(("blk", "head"), None)
    return jax.shard_map(per_device, mesh=mesh, in_specs=in_specs, out_specs=out_specs, check_vma=False)
```

```python
import functools

import jax
import jax.numpy as jnp
from jax import lax
from jax.experimental import pallas as pl
from jax.experimental.pallas import tpu as pltpu
from jax.sharding import PartitionSpec as P

HEADS = 32
KV_HEADS = 8
HD = 128
LANES = 128
LOG2E = 1.4426950408889634
NEG = -1e30
BF = jnp.bfloat16
F32 = jnp.float32


def params(mebibytes):
    return pltpu.CompilerParams(vmem_limit_bytes=mebibytes * 2**20)


def vmem_spec():
    return pl.BlockSpec(memory_space=pltpu.VMEM)


def smem_spec():
    return pl.BlockSpec(memory_space=pltpu.SMEM)


def fold_lanes(pieces):
    return jnp.sum(functools.reduce(jnp.add, pieces), axis=-1, keepdims=True)


def normalise(pieces, gain, epsilon):
    width = len(pieces) * pieces[0].shape[-1]
    mean = fold_lanes(pieces) / width
    centred = [piece - mean for piece in pieces]
    spread = fold_lanes([piece * piece for piece in centred]) / width
    factor = lax.rsqrt(spread + epsilon)
    return [(piece * factor * gain[index : index + 1, :]).astype(BF) for index, piece in enumerate(centred)]


def fixed(array):
    return pltpu.with_memory_space_constraint(array, pltpu.HBM)


def lane_rows(vector):
    return vector.reshape(-1, LANES)


def mlp_kernel(pages_hbm, dw_hbm, dwb_hbm, gain_hbm, w1_hbm, b1_hbm, w2_hbm, out, *scratch):
    padded, conv, pages, dw, dwb, gain, w1, b1, w2, arrived = scratch
    pairs = (
        (w1_hbm, w1),
        (w2_hbm, w2),
        (b1_hbm, b1),
        (gain_hbm, gain),
        (dwb_hbm, dwb),
        (dw_hbm, dw),
        (pages_hbm, pages),
    )
    loads = [pltpu.make_async_copy(source, target, arrived.at[index]) for index, (source, target) in enumerate(pairs)]
    for load in reversed(loads):
        load.start()
    for load in loads[2:]:
        load.wait()
    height, breadth, channels = pages.shape
    half = height // 2
    column = lax.broadcasted_iota(jnp.int32, (half, breadth, LANES), 1)
    blank = jnp.zeros((3, breadth, LANES), F32)
    for chunk in range(channels // LANES):
        lanes = slice(chunk * LANES, (chunk + 1) * LANES)
        padded[chunk, 0:3] = blank
        padded[chunk, 3 + height : 6 + height] = blank
        padded[chunk, 3 : 3 + height] = pages[:, :, lanes].astype(F32)
        for top in range(0, height, half):
            total = jnp.broadcast_to(dwb[chunk : chunk + 1, :][None], (half, breadth, LANES))
            for sideways in range(7):
                product = None
                for vertical in range(7):
                    tap = dw[vertical, sideways : sideways + 1, lanes][None]
                    term = padded[chunk, top + vertical : top + vertical + half] * tap
                    product = term if product is None else product + term
                offset = sideways - 3
                if offset:
                    rolled = pltpu.roll(product, (-offset) % breadth, axis=1)
                    inside = (column + offset >= 0) if offset < 0 else (column + offset < breadth)
                    product = jnp.where(inside, rolled, 0.0)
                total = total + product
            conv[chunk, top * breadth : (top + half) * breadth] = total.reshape(half * breadth, LANES)
    normed = normalise([conv[chunk] for chunk in range(channels // LANES)], gain, 1e-06)
    loads[0].wait()
    product = jnp.dot(jnp.concatenate(normed, axis=1), w1[...], preferred_element_type=F32)
    hidden = []
    for chunk in range(product.shape[1] // LANES):
        pre = product[:, chunk * LANES : (chunk + 1) * LANES] + b1[chunk : chunk + 1, :]
        hidden.append((0.5 * pre * (1.0 + lax.erf(pre * 0.7071067811865476))).astype(BF))
    loads[1].wait()
    out[...] = jnp.dot(jnp.concatenate(hidden, axis=1), w2[...], preferred_element_type=F32).astype(BF)


def mlp(pages, dw, dwb, gain, w1, b1, w2):
    _, height, breadth, channels = pages.shape
    rows = height * breadth
    operands = (pages[0], dw, lane_rows(dwb), lane_rows(gain), w1, lane_rows(b1), w2)
    return pl.pallas_call(
        mlp_kernel,
        out_shape=jax.ShapeDtypeStruct((rows, channels), BF),
        in_specs=[pl.BlockSpec(memory_space=pltpu.HBM)] * 7,
        out_specs=vmem_spec(),
        scratch_shapes=[
            pltpu.VMEM((channels // LANES, height + 6, breadth, LANES), F32),
            pltpu.VMEM((channels // LANES, rows, LANES), F32),
            *[pltpu.VMEM(operand.shape, operand.dtype) for operand in operands],
            pltpu.SemaphoreType.DMA((7,)),
        ],
        compiler_params=params(16),
        name="conv_mlp",
    )(*[fixed(operand) for operand in operands])


def block_kernel(place, parts, pages, packed, out):
    count, chunk, channels = parts.shape
    pieces = channels // LANES
    scale, b2 = packed[0:pieces, :], packed[pieces : 2 * pieces, :]
    start = pl.multiple_of(place[0] * chunk, chunk)
    block = []
    for index in range(channels // LANES):
        lanes = slice(index * LANES, (index + 1) * LANES)
        row = slice(index, index + 1)
        total = functools.reduce(jnp.add, [parts[part, :, lanes].astype(F32) for part in range(count)])
        own = pages[pl.ds(start, chunk), lanes].astype(F32)
        block.append(own + scale[row, :] * (total + b2[row, :]))
    normed = jnp.concatenate(normalise(block, packed.at[2 * pieces : 3 * pieces, :], 1e-05), axis=1)
    for part in range(count):
        out[part] = normed


def block_norm(place, parts, pages, scale, b2, gain):
    return pl.pallas_call(
        block_kernel,
        out_shape=jax.ShapeDtypeStruct(parts.shape, BF),
        in_specs=[smem_spec()] + [vmem_spec()] * 3,
        out_specs=vmem_spec(),
        compiler_params=params(8),
        name="block_norm",
    )(place, parts, pages, jnp.concatenate([lane_rows(scale), lane_rows(b2), lane_rows(gain)]))


def kv_kernel(normed, wk, wv, out):
    tokens = normed[...]
    out[0, :, 0:HD] = jnp.dot(tokens, wv[...], preferred_element_type=F32).astype(BF)
    out[0, :, HD : 2 * HD] = jnp.dot(tokens, wk[...], preferred_element_type=F32).astype(BF)


def key_values(normed, wk, wv):
    rows = normed.shape[0]
    return pl.pallas_call(
        kv_kernel,
        out_shape=jax.ShapeDtypeStruct((1, rows, 2 * HD), BF),
        in_specs=[vmem_spec()] * 3,
        out_specs=vmem_spec(),
        compiler_params=params(8),
        name="key_values",
    )(normed, wk, wv)


def query_kernel(_, normed, wq, out):
    product = jnp.dot(normed[...], wq[...], preferred_element_type=F32) * (HD**-0.5 * LOG2E)
    for head in range(out.shape[0]):
        out[head] = product[:, head * HD : (head + 1) * HD].astype(BF)


def queries_of(valid_counts, normed, wq):
    rows = normed.shape[0]
    return pl.pallas_call(
        query_kernel,
        out_shape=jax.ShapeDtypeStruct((wq.shape[1] // HD, rows, HD), BF),
        in_specs=[smem_spec()] + [vmem_spec()] * 2,
        out_specs=vmem_spec(),
        compiler_params=params(8),
        name="queries",
    )(valid_counts, normed, wq)


def attend_kernel(first, last, places, depth, sizes, *refs):
    refs = list(refs)
    valid_counts, own = refs.pop(0), refs.pop(0)
    query = refs.pop(0)
    chunks = [refs.pop(0) for _ in sizes]
    if not first:
        top_in, sums_in = refs.pop(0), refs.pop(0)
    if last:
        w_out = refs.pop(0)
        mixed = refs.pop(0)
        top_out, sums_out = refs.pop(0), refs.pop(0)
    else:
        top_out, sums_out = refs.pop(0), refs.pop(0)
    heads, rows, _ = query.shape
    here = own[0]
    here_y, here_z, here_core = lax.div(here, 2 * depth), lax.rem(lax.div(here, 2), depth), lax.rem(here, 2)
    behind = 2 * here_core - 1
    pages = []
    for chunk, size in zip(chunks, sizes):
        for index in range(size):
            side, shift, core = places[len(pages)]
            place = lax.rem(here_z + depth + shift * behind, depth)
            number = (here_y ^ side) * (2 * depth) + place * 2 + (here_core ^ core)
            pages.append((chunk, index, valid_counts[number]))
    group_size = 4 if len(pages) in (4, 7, 8) else min(3, len(pages))
    tokens = chunks[0].shape[1]
    lane = lax.broadcasted_iota(jnp.int32, (1, tokens), 1)
    lane_kv = lax.broadcasted_iota(jnp.int32, (tokens, 2 * HD), 1)
    fresh = first
    for begin in range(0, len(pages), group_size):
        group = pages[begin : begin + group_size]
        keys, values, masks = [], [], []
        for chunk, index, count in group:
            both = chunk[index]
            keys.append(both[:, HD : 2 * HD])
            values.append(jnp.where(lane_kv < HD, both, jnp.ones_like(both)))
            masks.append(jnp.where(lane < count, 0.0, NEG).astype(F32))
        for head in range(heads):
            scores = [
                lax.dot_general(query[head], key, (((1,), (1,)), ((), ())), preferred_element_type=F32) + mask
                for key, mask in zip(keys, masks)
            ]
            largest = functools.reduce(jnp.maximum, scores)
            top = jnp.broadcast_to(jnp.max(largest, axis=1, keepdims=True), (rows, HD))
            if not fresh:
                source_top, source_sums = (top_in, sums_in) if begin == 0 else (top_out, sums_out)
                before = source_top[head]
                top = jnp.maximum(top, before)
                factor = jnp.exp2(before - top)
                carried = source_sums[head] * jnp.concatenate([factor, factor], axis=1)
            wide_top = jnp.concatenate([top] * (tokens // HD), axis=1)
            total = functools.reduce(
                jnp.add,
                [
                    jnp.dot(jnp.exp2(score - wide_top).astype(BF), value, preferred_element_type=F32)
                    for score, value in zip(scores, values)
                ],
            )
            if not fresh:
                total = total + carried
            sums_out[head] = total
            top_out[head] = top
        fresh = False
    if last:
        attended = jnp.concatenate(
            [(sums_out[head][:, 0:HD] / sums_out[head][:, HD : 2 * HD]).astype(BF) for head in range(heads)], axis=1
        )
        mixed[...] = jnp.dot(attended, w_out[...], preferred_element_type=F32).astype(BF)


def attend(valid_counts, own, depth, query, pieces, carry=None, w_out=None):
    heads, rows, _ = query.shape
    chunks = [piece[0] for piece in pieces]
    places = [place for piece in pieces for place in piece[1]]
    sizes = tuple(chunk.shape[0] for chunk in chunks)
    state = [jax.ShapeDtypeStruct((heads, rows, HD), F32), jax.ShapeDtypeStruct((heads, rows, 2 * HD), F32)]
    operands = [valid_counts, own, query, *chunks]
    if carry is not None:
        operands += list(carry)
    scratch = []
    if w_out is not None:
        operands.append(w_out)
        out_shape = [jax.ShapeDtypeStruct((rows, w_out.shape[1]), BF)]
        scratch = [pltpu.VMEM(one.shape, F32) for one in state]
    else:
        out_shape = state
    pairs = sum(sizes) * chunks[0].shape[1] * heads * rows
    return pl.pallas_call(
        functools.partial(attend_kernel, carry is None, w_out is not None, places, depth, sizes),
        out_shape=out_shape,
        in_specs=[smem_spec()] * 2 + [vmem_spec()] * (len(operands) - 2),
        out_specs=[vmem_spec()] * len(out_shape),
        scratch_shapes=scratch,
        cost_estimate=pl.CostEstimate(flops=pairs // 8, transcendentals=0, bytes_accessed=2**16),
        compiler_params=params(14),
        name="attend",
    )(*operands)


def total_kernel(parts, out):
    total = parts[0].astype(F32)
    for part in range(1, parts.shape[0]):
        total = total + parts[part].astype(F32)
    out[...] = total.astype(BF)


def total_of(parts):
    return pl.pallas_call(
        total_kernel,
        out_shape=jax.ShapeDtypeStruct(parts.shape[1:], BF),
        in_specs=[vmem_spec()],
        out_specs=vmem_spec(),
        compiler_params=params(8),
        name="total",
    )(parts)


def per_device(
    pages,
    valid_counts,
    dw_weight,
    dw_bias,
    norm1_gain,
    fc1_w,
    fc1_b,
    fc2_w,
    fc2_b,
    layer_scale,
    norm2_gain,
    w_query,
    w_key,
    w_value,
    w_out,
):
    channels = pages.shape[-1]
    rows = pages.shape[1] * pages.shape[2]
    groups = lax.axis_size("head")
    blocks = lax.axis_size("blk")
    depth = blocks // 4
    share = rows // groups

    def moved(array, target):
        return lax.ppermute(array, "blk", [(i, target(i)) for i in range(blocks)])

    def flip_y(array):
        return moved(array, lambda i: (i + 2 * depth) % blocks)

    def flip_core(array):
        return moved(array, lambda i: i ^ 1)

    def along_z(array, step=1):
        def target(i):
            turn = 2 * step if i % 2 == 0 else -2 * step
            return i // (2 * depth) * (2 * depth) + (i + turn) % (2 * depth)

        return moved(array, target)

    own = lax.axis_index("blk").astype(jnp.int32)[None]
    place = lax.axis_index("head").astype(jnp.int32)[None]
    hold = lax.optimization_barrier

    partial = mlp(pages, dw_weight, dw_bias, norm1_gain, fc1_w, fc1_b, fc2_w)
    parts = lax.all_to_all(partial.reshape(groups, share, channels), "head", 0, 0, tiled=True)
    copies = block_norm(place, parts, pages.reshape(rows, channels), layer_scale, fc2_b, norm2_gain)
    normed = lax.all_to_all(copies, "head", 0, 0, tiled=True).reshape(rows, channels)

    def fold(pieces, carry=None, weight=None):
        return attend(valid_counts, own, depth, query, pieces, carry, weight)

    def crossed(places):
        return [(side, -shift, 1 - core) for side, shift, core in places]

    def both_cores(pieces, shared, carry, weight=None):
        exchanged = [flip_core(array) for array, _ in shared]
        carry = fold(pieces, carry)
        exchanged, carry = hold((exchanged, carry))
        return fold([(array, crossed(piece[1])) for array, piece in zip(exchanged, shared)], carry, weight)

    def halves(trio, places, single, place):
        joined = jnp.concatenate([trio[2:3], single])
        return [(trio[0:2], places[0:2]), (joined, [places[2], place])]

    start = key_values(normed, w_key, w_value)
    beside = flip_core(start)
    other = flip_y(start)
    query = queries_of(valid_counts, normed, w_query)
    beside, query = hold((beside, query))
    own_pair = jnp.concatenate([start, beside])

    one = jnp.concatenate([along_z(start), along_z(beside), other])
    carry = fold([(own_pair, [(0, 0, 0), (0, 0, 1)])])
    one, carry = hold((one, carry))

    two = along_z(one)
    one_other = flip_y(one[1:2])
    places = [(0, 1, 0), (0, 1, 1), (1, 0, 0)]
    shared = [(one[0:2], places[0:2]), (one[2:3], places[2:3])]
    carry = both_cores([(one, places)], shared, carry)
    two, one_other, carry = hold((two, one_other, carry))

    three = along_z(two)
    two_other = flip_y(two[1:2])
    places, place = [(0, 2, 0), (0, 2, 1), (1, 1, 0)], (1, 1, 1)
    carry = both_cores([(two, places), (one_other, [place])], halves(two, places, one_other, place), carry)
    three, two_other, carry = hold((three, two_other, carry))

    half = depth // 2
    four = along_z(three[1:3])
    three_other = flip_y(three[1:2])
    far_other = along_z(three[2:3], 2)
    joined = jnp.concatenate([three, two_other])
    pieces = [(joined, [(0, 3, 0), (0, 3, 1), (1, 2, 0), (1, 2, 1)])]
    carry = both_cores(pieces, pieces, carry)
    four, three_other, far_other, carry = hold((four, three_other, far_other, carry))

    joined = jnp.concatenate([four, three_other, far_other])
    pieces = [(joined, [(0, half, 1), (1, 3, 0), (1, 3, 1), (1, half, 0)])]
    (mixed,) = both_cores(pieces, pieces, carry, w_out)
    parts = lax.all_to_all(mixed.reshape(groups, share, channels), "head", 0, 0, tiled=True)
    return total_of(parts)


def solution(mesh):
    in_specs = (
        P("blk", None, None, None),
        P(),
        P(),
        P(),
        P(),
        P(None, "head"),
        P("head"),
        P("head", None),
        P(),
        P(),
        P(),
        P(None, "head"),
        P(None, "head"),
        P(None, "head"),
        P("head", None),
    )
    out_specs = P(("blk", "head"), None)
    return jax.shard_map(per_device, mesh=mesh, in_specs=in_specs, out_specs=out_specs, check_vma=False)
```

```python
import functools

import jax
import jax.numpy as jnp
from jax import lax
from jax.experimental import pallas as pl
from jax.experimental.pallas import tpu as pltpu
from jax.sharding import PartitionSpec as P

HEADS = 32
KV_HEADS = 8
HD = 128
LANES = 128
LOG2E = 1.4426950408889634
NEG = -1e30
BF = jnp.bfloat16
F32 = jnp.float32


def params(mebibytes):
    return pltpu.CompilerParams(vmem_limit_bytes=mebibytes * 2**20)


def vmem_spec():
    return pl.BlockSpec(memory_space=pltpu.VMEM)


def smem_spec():
    return pl.BlockSpec(memory_space=pltpu.SMEM)


def fold_lanes(pieces):
    return jnp.sum(functools.reduce(jnp.add, pieces), axis=-1, keepdims=True)


def normalise(pieces, gain, epsilon):
    width = len(pieces) * pieces[0].shape[-1]
    mean = fold_lanes(pieces) / width
    centred = [piece - mean for piece in pieces]
    spread = fold_lanes([piece * piece for piece in centred]) / width
    factor = lax.rsqrt(spread + epsilon)
    return [(piece * factor * gain[index : index + 1, :]).astype(BF) for index, piece in enumerate(centred)]


def fixed(array):
    return pltpu.with_memory_space_constraint(array, pltpu.HBM)


def lane_rows(vector):
    return vector.reshape(-1, LANES)


def mlp_kernel(pages_hbm, dw_hbm, dwb_hbm, gain_hbm, w1_hbm, b1_hbm, w2_hbm, out, *scratch):
    padded, conv, pages, dw, dwb, gain, w1, b1, w2, arrived = scratch
    chunks = pages.shape[2] // LANES
    pairs = [(dwb_hbm, dwb)]
    for chunk in range(chunks):
        lanes = slice(chunk * LANES, (chunk + 1) * LANES)
        pairs += [(pages_hbm.at[:, :, lanes], pages.at[:, :, lanes]), (dw_hbm.at[:, :, lanes], dw.at[:, :, lanes])]
    pairs += [(gain_hbm, gain), (b1_hbm, b1), (w1_hbm, w1), (w2_hbm, w2)]
    loads = [pltpu.make_async_copy(source, target, arrived.at[index]) for index, (source, target) in enumerate(pairs)]
    for load in loads:
        load.start()
    loads[0].wait()
    height, breadth, channels = pages.shape
    half = height // 2
    column = lax.broadcasted_iota(jnp.int32, (half, breadth, LANES), 1)
    blank = jnp.zeros((3, breadth, LANES), F32)
    for chunk in range(channels // LANES):
        lanes = slice(chunk * LANES, (chunk + 1) * LANES)
        loads[1 + 2 * chunk].wait()
        loads[2 + 2 * chunk].wait()
        padded[chunk, 0:3] = blank
        padded[chunk, 3 + height : 6 + height] = blank
        padded[chunk, 3 : 3 + height] = pages[:, :, lanes].astype(F32)
        for top in range(0, height, half):
            total = jnp.broadcast_to(dwb[chunk : chunk + 1, :][None], (half, breadth, LANES))
            for sideways in range(7):
                product = None
                for vertical in range(7):
                    tap = dw[vertical, sideways : sideways + 1, lanes][None]
                    term = padded[chunk, top + vertical : top + vertical + half] * tap
                    product = term if product is None else product + term
                offset = sideways - 3
                if offset:
                    rolled = pltpu.roll(product, (-offset) % breadth, axis=1)
                    inside = (column + offset >= 0) if offset < 0 else (column + offset < breadth)
                    product = jnp.where(inside, rolled, 0.0)
                total = total + product
            conv[chunk, top * breadth : (top + half) * breadth] = total.reshape(half * breadth, LANES)
    loads[-4].wait()
    normed = normalise([conv[chunk] for chunk in range(channels // LANES)], gain, 1e-06)
    loads[-3].wait()
    loads[-2].wait()
    product = jnp.dot(jnp.concatenate(normed, axis=1), w1[...], preferred_element_type=F32)
    hidden = []
    for chunk in range(product.shape[1] // LANES):
        pre = product[:, chunk * LANES : (chunk + 1) * LANES] + b1[chunk : chunk + 1, :]
        hidden.append((0.5 * pre * (1.0 + lax.erf(pre * 0.7071067811865476))).astype(BF))
    loads[-1].wait()
    out[...] = jnp.dot(jnp.concatenate(hidden, axis=1), w2[...], preferred_element_type=F32).astype(BF)


def mlp(pages, dw, dwb, gain, w1, b1, w2):
    _, height, breadth, channels = pages.shape
    rows = height * breadth
    operands = (pages[0], dw, lane_rows(dwb), lane_rows(gain), w1, lane_rows(b1), w2)
    return pl.pallas_call(
        mlp_kernel,
        out_shape=jax.ShapeDtypeStruct((rows, channels), BF),
        in_specs=[pl.BlockSpec(memory_space=pltpu.HBM)] * 7,
        out_specs=vmem_spec(),
        scratch_shapes=[
            pltpu.VMEM((channels // LANES, height + 6, breadth, LANES), F32),
            pltpu.VMEM((channels // LANES, rows, LANES), F32),
            *[pltpu.VMEM(operand.shape, operand.dtype) for operand in operands],
            pltpu.SemaphoreType.DMA((2 * (channels // LANES) + 5,)),
        ],
        compiler_params=params(16),
        name="conv_mlp",
    )(*[fixed(operand) for operand in operands])


def block_kernel(place, parts, pages, packed, out):
    count, chunk, channels = parts.shape
    pieces = channels // LANES
    scale, b2 = packed[0:pieces, :], packed[pieces : 2 * pieces, :]
    start = pl.multiple_of(place[0] * chunk, chunk)
    block = []
    for index in range(channels // LANES):
        lanes = slice(index * LANES, (index + 1) * LANES)
        row = slice(index, index + 1)
        total = functools.reduce(jnp.add, [parts[part, :, lanes].astype(F32) for part in range(count)])
        own = pages[pl.ds(start, chunk), lanes].astype(F32)
        block.append(own + scale[row, :] * (total + b2[row, :]))
    normed = jnp.concatenate(normalise(block, packed.at[2 * pieces : 3 * pieces, :], 1e-05), axis=1)
    for part in range(count):
        out[part] = normed


def block_norm(place, parts, pages, scale, b2, gain):
    return pl.pallas_call(
        block_kernel,
        out_shape=jax.ShapeDtypeStruct(parts.shape, BF),
        in_specs=[smem_spec()] + [vmem_spec()] * 3,
        out_specs=vmem_spec(),
        compiler_params=params(8),
        name="block_norm",
    )(place, parts, pages, jnp.concatenate([lane_rows(scale), lane_rows(b2), lane_rows(gain)]))


def kv_kernel(normed, wk, wv, out):
    tokens = normed[...]
    out[0, :, 0:HD] = jnp.dot(tokens, wv[...], preferred_element_type=F32).astype(BF)
    out[0, :, HD : 2 * HD] = jnp.dot(tokens, wk[...], preferred_element_type=F32).astype(BF)


def key_values(normed, wk, wv):
    rows = normed.shape[0]
    return pl.pallas_call(
        kv_kernel,
        out_shape=jax.ShapeDtypeStruct((1, rows, 2 * HD), BF),
        in_specs=[vmem_spec()] * 3,
        out_specs=vmem_spec(),
        compiler_params=params(8),
        name="key_values",
    )(normed, wk, wv)


def query_kernel(_, normed, wq, out):
    product = jnp.dot(normed[...], wq[...], preferred_element_type=F32) * (HD**-0.5 * LOG2E)
    for head in range(out.shape[0]):
        out[head] = product[:, head * HD : (head + 1) * HD].astype(BF)


def queries_of(valid_counts, normed, wq):
    rows = normed.shape[0]
    return pl.pallas_call(
        query_kernel,
        out_shape=jax.ShapeDtypeStruct((wq.shape[1] // HD, rows, HD), BF),
        in_specs=[smem_spec()] + [vmem_spec()] * 2,
        out_specs=vmem_spec(),
        compiler_params=params(8),
        name="queries",
    )(valid_counts, normed, wq)


def attend_kernel(first, last, places, depth, sizes, *refs):
    refs = list(refs)
    valid_counts, own = refs.pop(0), refs.pop(0)
    query = refs.pop(0)
    chunks = [refs.pop(0) for _ in sizes]
    if not first:
        top_in, sums_in = refs.pop(0), refs.pop(0)
    if last:
        w_out = refs.pop(0)
        mixed = refs.pop(0)
        top_out, sums_out = refs.pop(0), refs.pop(0)
    else:
        top_out, sums_out = refs.pop(0), refs.pop(0)
    heads, rows, _ = query.shape
    here = own[0]
    here_y, here_z, here_core = lax.div(here, 2 * depth), lax.rem(lax.div(here, 2), depth), lax.rem(here, 2)
    behind = 2 * here_core - 1
    pages = []
    for chunk, size in zip(chunks, sizes):
        for index in range(size):
            side, shift, core = places[len(pages)]
            place = lax.rem(here_z + depth + shift * behind, depth)
            number = (here_y ^ side) * (2 * depth) + place * 2 + (here_core ^ core)
            pages.append((chunk, index, valid_counts[number]))
    group_size = 4 if len(pages) in (4, 7, 8) else min(3, len(pages))
    tokens = chunks[0].shape[1]
    lane = lax.broadcasted_iota(jnp.int32, (1, tokens), 1)
    lane_kv = lax.broadcasted_iota(jnp.int32, (tokens, 2 * HD), 1)
    fresh = first
    for begin in range(0, len(pages), group_size):
        group = pages[begin : begin + group_size]
        keys, values, masks = [], [], []
        for chunk, index, count in group:
            both = chunk[index]
            keys.append(both[:, HD : 2 * HD])
            values.append(jnp.where(lane_kv < HD, both, jnp.ones_like(both)))
            masks.append(jnp.where(lane < count, 0.0, NEG).astype(F32))
        for head in range(heads):
            scores = [
                lax.dot_general(query[head], key, (((1,), (1,)), ((), ())), preferred_element_type=F32) + mask
                for key, mask in zip(keys, masks)
            ]
            largest = functools.reduce(jnp.maximum, scores)
            top = jnp.broadcast_to(jnp.max(largest, axis=1, keepdims=True), (rows, HD))
            if not fresh:
                source_top, source_sums = (top_in, sums_in) if begin == 0 else (top_out, sums_out)
                before = source_top[head]
                top = jnp.maximum(top, before)
                factor = jnp.exp2(before - top)
                carried = source_sums[head] * jnp.concatenate([factor, factor], axis=1)
            wide_top = jnp.concatenate([top] * (tokens // HD), axis=1)
            total = functools.reduce(
                jnp.add,
                [
                    jnp.dot(jnp.exp2(score - wide_top).astype(BF), value, preferred_element_type=F32)
                    for score, value in zip(scores, values)
                ],
            )
            if not fresh:
                total = total + carried
            sums_out[head] = total
            top_out[head] = top
        fresh = False
    if last:
        attended = jnp.concatenate(
            [(sums_out[head][:, 0:HD] / sums_out[head][:, HD : 2 * HD]).astype(BF) for head in range(heads)], axis=1
        )
        mixed[...] = jnp.dot(attended, w_out[...], preferred_element_type=F32).astype(BF)


def attend(valid_counts, own, depth, query, pieces, carry=None, w_out=None):
    heads, rows, _ = query.shape
    chunks = [piece[0] for piece in pieces]
    places = [place for piece in pieces for place in piece[1]]
    sizes = tuple(chunk.shape[0] for chunk in chunks)
    state = [jax.ShapeDtypeStruct((heads, rows, HD), F32), jax.ShapeDtypeStruct((heads, rows, 2 * HD), F32)]
    operands = [valid_counts, own, query, *chunks]
    if carry is not None:
        operands += list(carry)
    scratch = []
    if w_out is not None:
        operands.append(w_out)
        out_shape = [jax.ShapeDtypeStruct((rows, w_out.shape[1]), BF)]
        scratch = [pltpu.VMEM(one.shape, F32) for one in state]
    else:
        out_shape = state
    pairs = sum(sizes) * chunks[0].shape[1] * heads * rows
    return pl.pallas_call(
        functools.partial(attend_kernel, carry is None, w_out is not None, places, depth, sizes),
        out_shape=out_shape,
        in_specs=[smem_spec()] * 2 + [vmem_spec()] * (len(operands) - 2),
        out_specs=[vmem_spec()] * len(out_shape),
        scratch_shapes=scratch,
        cost_estimate=pl.CostEstimate(flops=pairs // 8, transcendentals=0, bytes_accessed=2**16),
        compiler_params=params(14),
        name="attend",
    )(*operands)


def total_kernel(parts, out):
    total = parts[0].astype(F32)
    for part in range(1, parts.shape[0]):
        total = total + parts[part].astype(F32)
    out[...] = total.astype(BF)


def total_of(parts):
    return pl.pallas_call(
        total_kernel,
        out_shape=jax.ShapeDtypeStruct(parts.shape[1:], BF),
        in_specs=[vmem_spec()],
        out_specs=vmem_spec(),
        compiler_params=params(8),
        name="total",
    )(parts)


def per_device(
    pages,
    valid_counts,
    dw_weight,
    dw_bias,
    norm1_gain,
    fc1_w,
    fc1_b,
    fc2_w,
    fc2_b,
    layer_scale,
    norm2_gain,
    w_query,
    w_key,
    w_value,
    w_out,
):
    channels = pages.shape[-1]
    rows = pages.shape[1] * pages.shape[2]
    groups = lax.axis_size("head")
    blocks = lax.axis_size("blk")
    depth = blocks // 4
    share = rows // groups

    def moved(array, target):
        return lax.ppermute(array, "blk", [(i, target(i)) for i in range(blocks)])

    def flip_y(array):
        return moved(array, lambda i: (i + 2 * depth) % blocks)

    def flip_core(array):
        return moved(array, lambda i: i ^ 1)

    def along_z(array, step=1):
        def target(i):
            turn = 2 * step if i % 2 == 0 else -2 * step
            return i // (2 * depth) * (2 * depth) + (i + turn) % (2 * depth)

        return moved(array, target)

    own = lax.axis_index("blk").astype(jnp.int32)[None]
    place = lax.axis_index("head").astype(jnp.int32)[None]
    hold = lax.optimization_barrier

    partial = mlp(pages, dw_weight, dw_bias, norm1_gain, fc1_w, fc1_b, fc2_w)
    parts = lax.all_to_all(partial.reshape(groups, share, channels), "head", 0, 0, tiled=True)
    copies = block_norm(place, parts, pages.reshape(rows, channels), layer_scale, fc2_b, norm2_gain)
    normed = lax.all_to_all(copies, "head", 0, 0, tiled=True).reshape(rows, channels)

    def fold(pieces, carry=None, weight=None):
        return attend(valid_counts, own, depth, query, pieces, carry, weight)

    def crossed(places):
        return [(side, -shift, 1 - core) for side, shift, core in places]

    def both_cores(pieces, shared, carry, weight=None):
        exchanged = [flip_core(array) for array, _ in shared]
        carry = fold(pieces, carry)
        exchanged, carry = hold((exchanged, carry))
        return fold([(array, crossed(piece[1])) for array, piece in zip(exchanged, shared)], carry, weight)

    def halves(trio, places, single, place):
        joined = jnp.concatenate([trio[2:3], single])
        return [(trio[0:2], places[0:2]), (joined, [places[2], place])]

    start = key_values(normed, w_key, w_value)
    beside = flip_core(start)
    other = flip_y(start)
    own_pair = jnp.concatenate([start, beside])
    own_pair, later = hold((own_pair, normed))
    query = queries_of(valid_counts, later, w_query)

    one = along_z(own_pair)
    carry = fold([(own_pair, [(0, 0, 0), (0, 0, 1)])])
    one, other, carry = hold((one, other, carry))

    two = along_z(jnp.concatenate([one, other]))
    one_other = flip_y(one[1:2])
    pieces = [(one, [(0, 1, 0), (0, 1, 1)]), (other, [(1, 0, 0)])]
    carry = both_cores(pieces, pieces, carry)
    two, one_other, carry = hold((two, one_other, carry))

    three = along_z(two)
    two_other = flip_y(two[1:2])
    places, place = [(0, 2, 0), (0, 2, 1), (1, 1, 0)], (1, 1, 1)
    carry = both_cores([(two, places), (one_other, [place])], halves(two, places, one_other, place), carry)
    three, two_other, carry = hold((three, two_other, carry))

    half = depth // 2
    four = along_z(three[1:3])
    three_other = flip_y(three[1:2])
    far_other = along_z(three[2:3], 2)
    joined = jnp.concatenate([three, two_other])
    pieces = [(joined, [(0, 3, 0), (0, 3, 1), (1, 2, 0), (1, 2, 1)])]
    carry = both_cores(pieces, pieces, carry)
    four, three_other, far_other, carry = hold((four, three_other, far_other, carry))

    joined = jnp.concatenate([four, three_other, far_other])
    pieces = [(joined, [(0, half, 1), (1, 3, 0), (1, 3, 1), (1, half, 0)])]
    (mixed,) = both_cores(pieces, pieces, carry, w_out)
    parts = lax.all_to_all(mixed.reshape(groups, share, channels), "head", 0, 0, tiled=True)
    return total_of(parts)


def solution(mesh):
    in_specs = (
        P("blk", None, None, None),
        P(),
        P(),
        P(),
        P(),
        P(None, "head"),
        P("head"),
        P("head", None),
        P(),
        P(),
        P(),
        P(None, "head"),
        P(None, "head"),
        P(None, "head"),
        P("head", None),
    )
    out_specs = P(("blk", "head"), None)
    return jax.shard_map(per_device, mesh=mesh, in_specs=in_specs, out_specs=out_specs, check_vma=False)
```

```python
import functools

import jax
import jax.numpy as jnp
from jax import lax
from jax.experimental import pallas as pl
from jax.experimental.pallas import tpu as pltpu
from jax.sharding import PartitionSpec as P

HEADS = 32
KV_HEADS = 8
HD = 128
LANES = 128
LOG2E = 1.4426950408889634
NEG = -1e30
BF = jnp.bfloat16
F32 = jnp.float32


def params(mebibytes):
    return pltpu.CompilerParams(vmem_limit_bytes=mebibytes * 2**20)


def vmem_spec():
    return pl.BlockSpec(memory_space=pltpu.VMEM)


def smem_spec():
    return pl.BlockSpec(memory_space=pltpu.SMEM)


def fold_lanes(pieces):
    return jnp.sum(functools.reduce(jnp.add, pieces), axis=-1, keepdims=True)


def normalise(pieces, gain, epsilon):
    width = len(pieces) * pieces[0].shape[-1]
    mean = fold_lanes(pieces) / width
    centred = [piece - mean for piece in pieces]
    spread = fold_lanes([piece * piece for piece in centred]) / width
    factor = lax.rsqrt(spread + epsilon)
    return [(piece * factor * gain[index : index + 1, :]).astype(BF) for index, piece in enumerate(centred)]


def fixed(array):
    return pltpu.with_memory_space_constraint(array, pltpu.HBM)


def lane_rows(vector):
    return vector.reshape(-1, LANES)


def mlp_kernel(pages_hbm, dw_hbm, dwb_hbm, gain_hbm, w1_hbm, b1_hbm, w2_hbm, out, *scratch):
    padded, conv, pages, dw, dwb, gain, w1, b1, w2, arrived = scratch
    chunks = pages.shape[2] // LANES
    pairs = [(dwb_hbm, dwb)]
    for chunk in range(chunks):
        lanes = slice(chunk * LANES, (chunk + 1) * LANES)
        pairs += [(pages_hbm.at[:, :, lanes], pages.at[:, :, lanes]), (dw_hbm.at[:, :, lanes], dw.at[:, :, lanes])]
    pairs += [(gain_hbm, gain), (b1_hbm, b1), (w1_hbm, w1), (w2_hbm, w2)]
    loads = [pltpu.make_async_copy(source, target, arrived.at[index]) for index, (source, target) in enumerate(pairs)]
    for load in loads:
        load.start()
    loads[0].wait()
    height, breadth, channels = pages.shape
    half = height // 2
    column = lax.broadcasted_iota(jnp.int32, (breadth, LANES), 0)
    blank = jnp.zeros((3, breadth, LANES), F32)
    for chunk in range(channels // LANES):
        lanes = slice(chunk * LANES, (chunk + 1) * LANES)
        loads[1 + 2 * chunk].wait()
        loads[2 + 2 * chunk].wait()
        padded[chunk, 0:3] = blank
        padded[chunk, 3 + height : 6 + height] = blank
        padded[chunk, 3 : 3 + height] = pages[:, :, lanes].astype(F32)
        taps = []
        for sideways in range(7):
            offset = sideways - 3
            inside = (column - offset >= 0) if offset > 0 else (column - offset < breadth)
            for vertical in range(7):
                tap = dw[vertical, sideways : sideways + 1, lanes]
                taps.append(jnp.where(inside, tap, 0.0)[None] if offset else tap[None])
        for top in range(0, height, half):
            total = jnp.broadcast_to(dwb[chunk : chunk + 1, :][None], (half, breadth, LANES))
            for sideways in range(7):
                product = None
                for vertical in range(7):
                    term = padded[chunk, top + vertical : top + vertical + half] * taps[7 * sideways + vertical]
                    product = term if product is None else product + term
                if sideways != 3:
                    product = pltpu.roll(product, (3 - sideways) % breadth, axis=1)
                total = total + product
            conv[chunk, top * breadth : (top + half) * breadth] = total.reshape(half * breadth, LANES)
    loads[-4].wait()
    normed = normalise([conv[chunk] for chunk in range(channels // LANES)], gain, 1e-06)
    loads[-3].wait()
    loads[-2].wait()
    product = jnp.dot(jnp.concatenate(normed, axis=1), w1[...], preferred_element_type=F32)
    hidden = []
    for chunk in range(product.shape[1] // LANES):
        pre = product[:, chunk * LANES : (chunk + 1) * LANES] + b1[chunk : chunk + 1, :]
        hidden.append((0.5 * pre * (1.0 + lax.erf(pre * 0.7071067811865476))).astype(BF))
    loads[-1].wait()
    out[...] = jnp.dot(jnp.concatenate(hidden, axis=1), w2[...], preferred_element_type=F32).astype(BF)


def mlp(pages, dw, dwb, gain, w1, b1, w2):
    _, height, breadth, channels = pages.shape
    rows = height * breadth
    operands = (pages[0], dw, lane_rows(dwb), lane_rows(gain), w1, lane_rows(b1), w2)
    return pl.pallas_call(
        mlp_kernel,
        out_shape=jax.ShapeDtypeStruct((rows, channels), BF),
        in_specs=[pl.BlockSpec(memory_space=pltpu.HBM)] * 7,
        out_specs=vmem_spec(),
        scratch_shapes=[
            pltpu.VMEM((channels // LANES, height + 6, breadth, LANES), F32),
            pltpu.VMEM((channels // LANES, rows, LANES), F32),
            *[pltpu.VMEM(operand.shape, operand.dtype) for operand in operands],
            pltpu.SemaphoreType.DMA((2 * (channels // LANES) + 5,)),
        ],
        compiler_params=params(16),
        name="conv_mlp",
    )(*[fixed(operand) for operand in operands])


def block_kernel(place, parts, pages, packed, out):
    count, chunk, channels = parts.shape
    pieces = channels // LANES
    scale, b2 = packed[0:pieces, :], packed[pieces : 2 * pieces, :]
    start = pl.multiple_of(place[0] * chunk, chunk)
    block = []
    for index in range(channels // LANES):
        lanes = slice(index * LANES, (index + 1) * LANES)
        row = slice(index, index + 1)
        total = functools.reduce(jnp.add, [parts[part, :, lanes].astype(F32) for part in range(count)])
        own = pages[pl.ds(start, chunk), lanes].astype(F32)
        block.append(own + scale[row, :] * (total + b2[row, :]))
    normed = jnp.concatenate(normalise(block, packed.at[2 * pieces : 3 * pieces, :], 1e-05), axis=1)
    for part in range(count):
        out[part] = normed


def block_norm(place, parts, pages, scale, b2, gain):
    return pl.pallas_call(
        block_kernel,
        out_shape=jax.ShapeDtypeStruct(parts.shape, BF),
        in_specs=[smem_spec()] + [vmem_spec()] * 3,
        out_specs=vmem_spec(),
        compiler_params=params(8),
        name="block_norm",
    )(place, parts, pages, jnp.concatenate([lane_rows(scale), lane_rows(b2), lane_rows(gain)]))


def kv_kernel(normed, wk, wv, out):
    tokens = normed[...]
    out[0, :, 0:HD] = jnp.dot(tokens, wv[...], preferred_element_type=F32).astype(BF)
    out[0, :, HD : 2 * HD] = jnp.dot(tokens, wk[...], preferred_element_type=F32).astype(BF)


def key_values(normed, wk, wv):
    rows = normed.shape[0]
    return pl.pallas_call(
        kv_kernel,
        out_shape=jax.ShapeDtypeStruct((1, rows, 2 * HD), BF),
        in_specs=[vmem_spec()] * 3,
        out_specs=vmem_spec(),
        compiler_params=params(8),
        name="key_values",
    )(normed, wk, wv)


def query_kernel(_, normed, wq, out):
    product = jnp.dot(normed[...], wq[...], preferred_element_type=F32) * (HD**-0.5 * LOG2E)
    for head in range(out.shape[0]):
        out[head] = product[:, head * HD : (head + 1) * HD].astype(BF)


def queries_of(valid_counts, normed, wq):
    rows = normed.shape[0]
    return pl.pallas_call(
        query_kernel,
        out_shape=jax.ShapeDtypeStruct((wq.shape[1] // HD, rows, HD), BF),
        in_specs=[smem_spec()] + [vmem_spec()] * 2,
        out_specs=vmem_spec(),
        compiler_params=params(8),
        name="queries",
    )(valid_counts, normed, wq)


def attend_kernel(first, last, places, depth, sizes, *refs):
    refs = list(refs)
    valid_counts, own = refs.pop(0), refs.pop(0)
    query = refs.pop(0)
    chunks = [refs.pop(0) for _ in sizes]
    if not first:
        top_in, sums_in = refs.pop(0), refs.pop(0)
    if last:
        w_out = refs.pop(0)
        mixed = refs.pop(0)
        top_out, sums_out = refs.pop(0), refs.pop(0)
    else:
        top_out, sums_out = refs.pop(0), refs.pop(0)
    heads, rows, _ = query.shape
    here = own[0]
    here_y, here_z, here_core = lax.div(here, 2 * depth), lax.rem(lax.div(here, 2), depth), lax.rem(here, 2)
    behind = 2 * here_core - 1
    pages = []
    for chunk, size in zip(chunks, sizes):
        for index in range(size):
            side, shift, core = places[len(pages)]
            place = lax.rem(here_z + depth + shift * behind, depth)
            number = (here_y ^ side) * (2 * depth) + place * 2 + (here_core ^ core)
            pages.append((chunk, index, valid_counts[number]))
    group_size = 4 if len(pages) in (4, 7, 8) else min(3, len(pages))
    tokens = chunks[0].shape[1]
    lane = lax.broadcasted_iota(jnp.int32, (1, tokens), 1)
    lane_kv = lax.broadcasted_iota(jnp.int32, (tokens, 2 * HD), 1)
    fresh = first
    for begin in range(0, len(pages), group_size):
        group = pages[begin : begin + group_size]
        keys, values, masks = [], [], []
        for chunk, index, count in group:
            both = chunk[index]
            keys.append(both[:, HD : 2 * HD])
            values.append(jnp.where(lane_kv < HD, both, jnp.ones_like(both)))
            masks.append(jnp.where(lane < count, 0.0, NEG).astype(F32))
        for head in range(heads):
            scores = [
                lax.dot_general(query[head], key, (((1,), (1,)), ((), ())), preferred_element_type=F32) + mask
                for key, mask in zip(keys, masks)
            ]
            largest = functools.reduce(jnp.maximum, scores)
            top = jnp.broadcast_to(jnp.max(largest, axis=1, keepdims=True), (rows, HD))
            if not fresh:
                source_top, source_sums = (top_in, sums_in) if begin == 0 else (top_out, sums_out)
                before = source_top[head]
                top = jnp.maximum(top, before)
                factor = jnp.exp2(before - top)
                carried = source_sums[head] * jnp.concatenate([factor, factor], axis=1)
            wide_top = jnp.concatenate([top] * (tokens // HD), axis=1)
            total = functools.reduce(
                jnp.add,
                [
                    jnp.dot(jnp.exp2(score - wide_top).astype(BF), value, preferred_element_type=F32)
                    for score, value in zip(scores, values)
                ],
            )
            if not fresh:
                total = total + carried
            sums_out[head] = total
            top_out[head] = top
        fresh = False
    if last:
        attended = jnp.concatenate(
            [(sums_out[head][:, 0:HD] / sums_out[head][:, HD : 2 * HD]).astype(BF) for head in range(heads)], axis=1
        )
        mixed[...] = jnp.dot(attended, w_out[...], preferred_element_type=F32).astype(BF)


def attend(valid_counts, own, depth, query, pieces, carry=None, w_out=None):
    heads, rows, _ = query.shape
    chunks = [piece[0] for piece in pieces]
    places = [place for piece in pieces for place in piece[1]]
    sizes = tuple(chunk.shape[0] for chunk in chunks)
    state = [jax.ShapeDtypeStruct((heads, rows, HD), F32), jax.ShapeDtypeStruct((heads, rows, 2 * HD), F32)]
    operands = [valid_counts, own, query, *chunks]
    if carry is not None:
        operands += list(carry)
    scratch = []
    if w_out is not None:
        operands.append(w_out)
        out_shape = [jax.ShapeDtypeStruct((rows, w_out.shape[1]), BF)]
        scratch = [pltpu.VMEM(one.shape, F32) for one in state]
    else:
        out_shape = state
    pairs = sum(sizes) * chunks[0].shape[1] * heads * rows
    return pl.pallas_call(
        functools.partial(attend_kernel, carry is None, w_out is not None, places, depth, sizes),
        out_shape=out_shape,
        in_specs=[smem_spec()] * 2 + [vmem_spec()] * (len(operands) - 2),
        out_specs=[vmem_spec()] * len(out_shape),
        scratch_shapes=scratch,
        cost_estimate=pl.CostEstimate(flops=pairs // 8, transcendentals=0, bytes_accessed=2**16),
        compiler_params=params(14),
        name="attend",
    )(*operands)


def total_kernel(parts, out):
    total = parts[0].astype(F32)
    for part in range(1, parts.shape[0]):
        total = total + parts[part].astype(F32)
    out[...] = total.astype(BF)


def total_of(parts):
    return pl.pallas_call(
        total_kernel,
        out_shape=jax.ShapeDtypeStruct(parts.shape[1:], BF),
        in_specs=[vmem_spec()],
        out_specs=vmem_spec(),
        compiler_params=params(8),
        name="total",
    )(parts)


def per_device(
    pages,
    valid_counts,
    dw_weight,
    dw_bias,
    norm1_gain,
    fc1_w,
    fc1_b,
    fc2_w,
    fc2_b,
    layer_scale,
    norm2_gain,
    w_query,
    w_key,
    w_value,
    w_out,
):
    channels = pages.shape[-1]
    rows = pages.shape[1] * pages.shape[2]
    groups = lax.axis_size("head")
    blocks = lax.axis_size("blk")
    depth = blocks // 4
    share = rows // groups

    def moved(array, target):
        return lax.ppermute(array, "blk", [(i, target(i)) for i in range(blocks)])

    def flip_y(array):
        return moved(array, lambda i: (i + 2 * depth) % blocks)

    def flip_core(array):
        return moved(array, lambda i: i ^ 1)

    def along_z(array, step=1):
        def target(i):
            turn = 2 * step if i % 2 == 0 else -2 * step
            return i // (2 * depth) * (2 * depth) + (i + turn) % (2 * depth)

        return moved(array, target)

    own = lax.axis_index("blk").astype(jnp.int32)[None]
    place = lax.axis_index("head").astype(jnp.int32)[None]
    hold = lax.optimization_barrier

    partial = mlp(pages, dw_weight, dw_bias, norm1_gain, fc1_w, fc1_b, fc2_w)
    parts = lax.all_to_all(partial.reshape(groups, share, channels), "head", 0, 0, tiled=True)
    copies = block_norm(place, parts, pages.reshape(rows, channels), layer_scale, fc2_b, norm2_gain)
    normed = lax.all_to_all(copies, "head", 0, 0, tiled=True).reshape(rows, channels)

    def fold(pieces, carry=None, weight=None):
        return attend(valid_counts, own, depth, query, pieces, carry, weight)

    def crossed(places):
        return [(side, -shift, 1 - core) for side, shift, core in places]

    def both_cores(pieces, shared, carry, weight=None):
        exchanged = [flip_core(array) for array, _ in shared]
        carry = fold(pieces, carry)
        exchanged, carry = hold((exchanged, carry))
        return fold([(array, crossed(piece[1])) for array, piece in zip(exchanged, shared)], carry, weight)

    def halves(trio, places, single, place):
        joined = jnp.concatenate([trio[2:3], single])
        return [(trio[0:2], places[0:2]), (joined, [places[2], place])]

    start = key_values(normed, w_key, w_value)
    beside = flip_core(start)
    other = flip_y(start)
    own_pair = jnp.concatenate([start, beside])
    own_pair, later = hold((own_pair, normed))
    query = queries_of(valid_counts, later, w_query)

    one = along_z(own_pair)
    carry = fold([(own_pair, [(0, 0, 0), (0, 0, 1)])])
    one, other, carry = hold((one, other, carry))

    two = along_z(jnp.concatenate([one, other]))
    one_other = flip_y(one[1:2])
    pieces = [(one, [(0, 1, 0), (0, 1, 1)]), (other, [(1, 0, 0)])]
    carry = both_cores(pieces, pieces, carry)
    two, one_other, carry = hold((two, one_other, carry))

    three = along_z(two)
    two_other = flip_y(two[1:2])
    places, place = [(0, 2, 0), (0, 2, 1), (1, 1, 0)], (1, 1, 1)
    carry = both_cores([(two, places), (one_other, [place])], halves(two, places, one_other, place), carry)
    three, two_other, carry = hold((three, two_other, carry))

    half = depth // 2
    four = along_z(three[1:3])
    three_other = flip_y(three[1:2])
    far_other = along_z(three[2:3], 2)
    joined = jnp.concatenate([three, two_other])
    pieces = [(joined, [(0, 3, 0), (0, 3, 1), (1, 2, 0), (1, 2, 1)])]
    carry = both_cores(pieces, pieces, carry)
    four, three_other, far_other, carry = hold((four, three_other, far_other, carry))

    joined = jnp.concatenate([four, three_other, far_other])
    pieces = [(joined, [(0, half, 1), (1, 3, 0), (1, 3, 1), (1, half, 0)])]
    (mixed,) = both_cores(pieces, pieces, carry, w_out)
    parts = lax.all_to_all(mixed.reshape(groups, share, channels), "head", 0, 0, tiled=True)
    return total_of(parts)


def solution(mesh):
    in_specs = (
        P("blk", None, None, None),
        P(),
        P(),
        P(),
        P(),
        P(None, "head"),
        P("head"),
        P("head", None),
        P(),
        P(),
        P(),
        P(None, "head"),
        P(None, "head"),
        P(None, "head"),
        P("head", None),
    )
    out_specs = P(("blk", "head"), None)
    return jax.shard_map(per_device, mesh=mesh, in_specs=in_specs, out_specs=out_specs, check_vma=False)
```
